128 devices in a mesh: member: 8 (over z, x_hi), lon: 16 (over y, x_lo, core).
Axes of the slice: x: 4 (x_hi: 2, x_lo: 2; x = x_hi * 2 + x_lo), y: 4, z: 4, core: 2. Of those that a mesh axis runs over, the one named last changes fastest.
Arguments:
- latent: bfloat16 [16, 4, 720, 641], P('member', None, 'lon'), may hold values from -6 to 6
- member_seeds: int32 [16], P('member'), may hold values from 0 to 63
- member_table: bfloat16 [64, 641], replicated, may hold values from -6 to 6
- row_bands: int32 [4], replicated, may hold values from 0 to 15
- disco_basis: bfloat16 [16, 4, 7, 7], replicated, may hold values from -0.8984375 to 0.8984375
- w_disco: bfloat16 [2564, 641], replicated, may hold values from -0.125 to 0.125
- w_expand: bfloat16 [641, 1282], replicated, may hold values from -0.25 to 0.25
- w_reduce: bfloat16 [1282, 641], replicated, may hold values from -0.15625 to 0.15625
- w_decode: bfloat16 [641, 288], replicated, may hold values from -0.25 to 0.25
- target: bfloat16 [4, 720, 288], P(None, 'lon'), may hold values from -12 to 12
Outputs:
- latent_grad: bfloat16 [16, 4, 720, 641], P('member', None, 'lon')
- grad_disco: bfloat16 [2564, 641], replicated
- grad_expand: bfloat16 [641, 1282], replicated
- grad_reduce: bfloat16 [1282, 641], replicated
- grad_decode: bfloat16 [641, 288], replicated
The draws below stay inside these ranges and needn't reach their ends.
All inputs are finite; a program needn't handle non-finite values.
Results may differ from the reference program's by a relative error of at most 0.025.
Values may be sent and summed in bfloat16 or wider, within the bound.
A program may use at most 128 MiB of HBM per device.

```python
import math
import jax
import jax.numpy as jnp
from jax import lax

CH = 641
HID = 1282
OUTC = 288
BASES = 4
BANDS = 16
SEEDS = 64
ROWS = 4
MEMBERS = 16
LON = 720


def touch_ends(values, own_key, low, largest):
    extent = values.shape
    index_at = [jax.random.randint(jax.random.fold_in(own_key, axis), (), 0, extent[axis]) for axis in range(len(extent))]
    values = values.at[tuple(index_at)].set(low)
    longest = extent.index(max(extent))
    index_at[longest] = (index_at[longest] + 1) % extent[longest]
    return values.at[tuple(index_at)].set(largest)


def block_levels(key, extent, pieces, low, largest):
    level = 1.0
    for dim, shards_of in pieces:
        steps = jax.random.uniform(jax.random.fold_in(jax.random.fold_in(key, 6), dim), (shards_of,), jnp.float32, low / len(pieces), largest / len(pieces))
        level = level * jnp.repeat(jnp.exp(steps), extent[dim] // shards_of).reshape((-1,) + (1,) * (len(extent) - 1 - dim))
    return level


def noise(own_key, extent, scale, limit, shards=(), dtype=jnp.bfloat16):
    array = scale * jax.random.normal(own_key, extent, jnp.float32)
    if shards:
        array = array * block_levels(own_key, extent, shards, -0.22, 0.18)
    return jnp.clip(array, -limit, limit).astype(dtype)


def setup_inputs(seed: int = 0) -> dict:
    keys = jax.random.split(jax.random.key(seed), 11)
    latent = noise(keys[0], (MEMBERS, ROWS, LON, CH), 1.0, 6.0, ((0, 8), (2, 16)))
    member_seeds = touch_ends(jax.random.randint(keys[1], (MEMBERS,), 0, SEEDS), jax.random.fold_in(keys[1], 1), 0, SEEDS - 1).astype(jnp.int32)
    member_table = noise(keys[2], (SEEDS, CH), 1.0, 6.0)
    row_bands = touch_ends(jax.random.randint(keys[3], (ROWS,), 0, BANDS), jax.random.fold_in(keys[3], 1), 0, BANDS - 1).astype(jnp.int32)
    disco_basis = noise(keys[4], (BANDS, BASES, 7, 7), 0.15, 0.8984375)
    w_disco = noise(keys[5], (BASES * CH, CH), (BASES * CH) ** -0.5, 0.125)
    w_expand = noise(keys[6], (CH, HID), CH ** -0.5, 0.25)
    w_reduce = noise(keys[7], (HID, CH), HID ** -0.5, 0.15625)
    w_decode = noise(keys[8], (CH, OUTC), CH ** -0.5, 0.25)
    target = noise(keys[9], (ROWS, LON, OUTC), 2.0, 12.0, ((1, 16),))
    return dict(latent=latent, member_seeds=member_seeds, member_table=member_table, row_bands=row_bands, disco_basis=disco_basis, w_disco=w_disco, w_expand=w_expand, w_reduce=w_reduce, w_decode=w_decode, target=target)


stencil_reach = 3
smooth = 0.5

def smooth_slope(difference):
    return difference / jnp.sqrt(difference * difference + smooth * smooth)

def gelu_value(value):
    return jax.nn.gelu(value, approximate=True)

def wrap_lon(field):
    return jnp.concatenate([field[:, -stencil_reach:], field, field[:, :stencil_reach]], axis=1)

def spread_member(field, stencil):
    row_count = field.shape[0]
    lon_count = field.shape[1]
    widened = wrap_lon(field)
    padded = jnp.pad(widened, ((stencil_reach, stencil_reach), (0, 0), (0, 0)))
    summed = None
    for tap_row in range(7):
        band_rows = padded[tap_row:tap_row + row_count].astype(jnp.float32)
        window = jnp.stack([band_rows[:, tap_col:tap_col + lon_count] for tap_col in range(7)], axis=2)
        contrib = jnp.einsum('rwbc,rkb->rwkc', window, stencil[:, :, tap_row, :].astype(jnp.float32))
        summed = contrib if summed is None else summed + contrib
    out_shape = summed.shape
    return summed.astype(jnp.bfloat16).reshape(out_shape[0], out_shape[1], out_shape[2] * out_shape[3])

def collect_member(grad, stencil):
    row_count = grad.shape[0]
    lon_count = grad.shape[1]
    basis_count = stencil.shape[1]
    split = grad.reshape(row_count, lon_count, basis_count, grad.shape[2] // basis_count)
    widened = wrap_lon(split)
    padded = jnp.pad(widened, ((3, 3), (0, 0), (0, 0), (0, 0)))
    stencil_tall = jnp.pad(stencil, ((3, 3), (0, 0), (0, 0), (0, 0)))
    summed = None
    for tap_row in range(7):
        source = padded[6 - tap_row:6 - tap_row + row_count].astype(jnp.float32)
        tap_coef = stencil_tall[6 - tap_row:6 - tap_row + row_count, :, tap_row, :].astype(jnp.float32)
        window = jnp.stack([source[:, 6 - tap_col:6 - tap_col + lon_count] for tap_col in range(7)], axis=2)
        contrib = jnp.einsum('rwbkc,rkb->rwc', window, tap_coef)
        summed = contrib if summed is None else summed + contrib
    return summed

def reference(latent, member_seeds, member_table, row_bands, disco_basis, w_disco, w_expand, w_reduce, w_decode, target):
    member_count, row_count, lon_count, chan_count = latent.shape
    stencil = disco_basis[row_bands]
    offsets = member_table[member_seeds].astype(jnp.float32)
    seeded = (latent.astype(jnp.float32) + offsets[:, None, None, :]).astype(jnp.bfloat16)
    spread = lax.map(lambda field: spread_member(field, stencil), seeded)
    flat_rows = member_count * row_count * lon_count
    spread_rows = spread.reshape(flat_rows, -1)
    seeded_rows = seeded.reshape(flat_rows, chan_count)
    conv_out = jnp.dot(spread_rows, w_disco, preferred_element_type=jnp.float32)
    hidden_in = (seeded_rows.astype(jnp.float32) + conv_out).astype(jnp.bfloat16)
    pre_act = jnp.dot(hidden_in, w_expand, preferred_element_type=jnp.float32)
    gelu_out = gelu_value(pre_act).astype(jnp.bfloat16)
    mixed = (hidden_in.astype(jnp.float32) + jnp.dot(gelu_out, w_reduce, preferred_element_type=jnp.float32)).astype(jnp.bfloat16)
    fields = jnp.dot(mixed, w_decode, preferred_element_type=jnp.float32).astype(jnp.bfloat16)
    fields = fields.reshape(member_count, row_count, lon_count, -1).astype(jnp.float32)
    paired = jnp.zeros_like(fields)
    for other in range(member_count):
        paired = paired + smooth_slope(fields - fields[other][None])
    field_grad = (smooth_slope(fields - target.astype(jnp.float32)[None]) - paired / (member_count - 1)).astype(jnp.bfloat16)
    grad_rows = field_grad.reshape(flat_rows, -1)
    mixed_grad = jnp.dot(grad_rows, w_decode.T, preferred_element_type=jnp.float32).astype(jnp.bfloat16)
    gelu_grad = jnp.dot(mixed_grad, w_reduce.T, preferred_element_type=jnp.float32)
    unused, pullback = jax.vjp(gelu_value, pre_act)
    pre_grad = pullback(gelu_grad)[0].astype(jnp.bfloat16)
    hidden_grad = (mixed_grad.astype(jnp.float32) + jnp.dot(pre_grad, w_expand.T, preferred_element_type=jnp.float32)).astype(jnp.bfloat16)
    spread_grad = jnp.dot(hidden_grad, w_disco.T, preferred_element_type=jnp.float32).astype(jnp.bfloat16)
    spread_grad = spread_grad.reshape(member_count, row_count, lon_count, -1)
    carried = lax.map(lambda grad: collect_member(grad, stencil), spread_grad)
    latent_grad = (hidden_grad.astype(jnp.float32).reshape(member_count, row_count, lon_count, chan_count) + carried).astype(jnp.bfloat16)
    factor = 1.0 / math.sqrt(member_count * row_count * lon_count)
    grad_disco = (jnp.dot(spread_rows.T, hidden_grad, preferred_element_type=jnp.float32) * factor).astype(jnp.bfloat16)
    grad_expand = (jnp.dot(hidden_in.T, pre_grad, preferred_element_type=jnp.float32) * factor).astype(jnp.bfloat16)
    grad_reduce = (jnp.dot(gelu_out.T, mixed_grad, preferred_element_type=jnp.float32) * factor).astype(jnp.bfloat16)
    grad_decode = (jnp.dot(mixed.T, grad_rows, preferred_element_type=jnp.float32) * factor).astype(jnp.bfloat16)
    return (latent_grad, grad_disco, grad_expand, grad_reduce, grad_decode)
```

```python
import functools
import math

import jax
import jax.numpy as jnp
from jax import lax
from jax.experimental import pallas as pl
from jax.experimental.pallas import tpu as pltpu
from jax.sharding import PartitionSpec as P

MESH = pl.DeviceIdType.MESH
f32 = jnp.float32
bf16 = jnp.bfloat16

CH = 641
HID = 1282
OUTC = 288
WIDE = 2564
ROWS = 384
HALF = 192
TILES = 1920
PART = 320
AXES = (("x", "y", "z"), ("y", "z", "x"), ("z", "x", "y"))
OFF_DISCO, OFF_EXPAND, OFF_REDUCE, OFF_DECODE, OFF_TAIL = 0, 805, 1215, 1620, 1743
U_DISCO, U_EXPAND, U_REDUCE, U_DECODE = 161, 41, 81, 41


def place():
    member, lon = lax.axis_index("member"), lax.axis_index("lon")
    return {
        "x": (member % 2) * 2 + (lon // 2) % 2,
        "y": lon // 4,
        "z": member // 2,
        "c": lon % 2,
    }


def device(at):
    return (at["z"] * 2 + at["x"] // 2, at["y"] * 4 + (at["x"] % 2) * 2 + at["c"])


def moved(at, axis, step):
    there = dict(at)
    size = 2 if axis == "c" else 4
    there[axis] = lax.rem(at[axis] + step + size, size)
    return there


def iota(shape, dim):
    return lax.broadcasted_iota(jnp.int32, shape, dim)


def dot(a, b):
    return jnp.dot(a, b, preferred_element_type=f32)


def dot_nt(a, b):
    return lax.dot_general(a, b, (((1,), (1,)), ((), ())), preferred_element_type=f32)


def flat_tiles(value):
    return value.astype(bf16).reshape(value.shape[0] // 16, 16, 128)


class Copies:
    def __init__(self, send_sems, recv_sems):
        self.send_sems, self.recv_sems, self.count = send_sems, recv_sems, 0
        self.started = []

    def send(self, src, dst, to):
        copy = pltpu.make_async_remote_copy(
            src_ref=src,
            dst_ref=dst,
            send_sem=self.send_sems.at[self.count],
            recv_sem=self.recv_sems.at[self.count],
            device_id=to,
            device_id_type=MESH,
        )
        self.count += 1
        copy.start()
        self.started.append(copy)
        return copy

    def finish(self):
        for copy in self.started:
            copy.wait_send()


def pair_slopes(fv, og, tgt, me_h, lanes, rows):
    lo, width = lanes
    values = [fv[j, rows, lo : lo + width] for j in range(16)]
    sums = [None] * 16

    def slope(d):
        return d * lax.rsqrt(d * d + 0.25)

    for i in range(16):
        for j in range(i + 1, 16):
            s = slope(values[i] - values[j])
            sums[i] = s if sums[i] is None else sums[i] + s
            sums[j] = -s if sums[j] is None else sums[j] - s
    goal = tgt[:, lo : lo + width]
    keep = me_h
    for i in range(16):
        value = slope(values[i] - goal) - sums[i] * (1.0 / 15.0)
        og[i, rows, lo : lo + width] = jnp.where(keep, value, 0.0)


def step_kernel(
    latent,
    seeds,
    table,
    bands,
    basis,
    wd_any,
    we_any,
    wr_any,
    wo_any,
    target,
    lg,
    flat,
    wd,
    we,
    wr,
    wo,
    tk,
    tt,
    wide,
    hs,
    spread,
    spread_t,
    hid,
    hid_t,
    gp,
    act,
    act_t,
    mix,
    mix_t,
    halo_s,
    halo_r,
    fs,
    fr,
    fv,
    og,
    gs,
    gr,
    tp,
    fg,
    mg,
    pg,
    hg,
    sgs,
    ob,
    back_r,
    grads,
    r0,
    r1,
    r2,
    r3,
    send_sems,
    recv_sems,
    load_sems,
):
    at = place()
    me = lax.axis_index("member")
    lon = lax.axis_index("lon")
    left = (me, lax.rem(lon + 15, 16))
    right = (me, lax.rem(lon + 1, 16))
    core = at["c"]
    copies = Copies(send_sems, recv_sems)

    loads = []
    for i, (src, dst) in enumerate(((wd_any, wd), (we_any, we), (wr_any, wr), (wo_any, wo))):
        load = pltpu.make_async_copy(src, dst, load_sems.at[i])
        load.start()
        loads.append(load)

    sibling = device(moved(at, "c", 1))
    barrier = pltpu.get_barrier_semaphore()
    greet = [sibling, left, right]
    greet += [device(moved(at, axis, d)) for axis in "xyz" for d in (1, 2, 3)]
    greet += [(lax.rem(me + d, 8), lon) for d in range(1, 8)]
    for peer in greet:
        pl.semaphore_signal(barrier, inc=1, device_id=peer, device_id_type=MESH)

    wide[...] = jnp.zeros_like(wide)
    hs[...] = jnp.zeros_like(hs)
    for ref in (hid, mix, mg, hg):
        ref[:, 640:768] = jnp.zeros((ROWS, 128), bf16)
    for ref in (act, pg):
        ref[:, 1280:1408] = jnp.zeros((ROWS, 128), bf16)
    fg[:, 256:384] = jnp.zeros((ROWS, 128), bf16)
    for m in range(2):
        pick = jnp.where(iota((8, 64), 1) == seeds[m], 1.0, 0.0).astype(bf16)
        offset = dot(pick, table[...])[0:1]
        for s in range(4):
            value = (latent[m, s].astype(f32) + offset).astype(bf16)
            wide[m, s * 64 : s * 64 + 45, 0:CH] = value
            hs[m * HALF + s * 48 : m * HALF + s * 48 + 45, 0:CH] = value

    row = iota((16, 256), 0)
    col = iota((16, 256), 1)
    third = lax.shift_right_logical(row * 11, 5)
    spot = third * 64 + (row - third * 3)
    first_pick = jnp.where((row < 12) & (col == spot), 1.0, 0.0).astype(bf16)
    last_pick = jnp.where((row < 12) & (col == spot + 42), 1.0, 0.0).astype(bf16)
    for m in range(2):
        halo_s[0, m] = dot(first_pick, wide[m]).astype(bf16)
        halo_s[1, m] = dot(last_pick, wide[m]).astype(bf16)

    pl.semaphore_wait(barrier, len(greet))
    from_right = copies.send(halo_s.at[0], halo_r.at[0], left)
    from_left = copies.send(halo_s.at[1], halo_r.at[1], right)

    keep_rows = iota((48, 256), 0) < 45
    for r in range(4):
        taps = basis[bands[r]].astype(f32)
        lines = None
        for s in range(4):
            a = s - r + 3
            some = jnp.concatenate([taps[k, a : a + 1, :] for k in range(4)], axis=0)
            some = jnp.concatenate([some, jnp.zeros((4, 249), f32)], axis=1)
            some = pltpu.roll(some, (s * 64 - 3) % 256, 1)
            lines = some if lines is None else lines + some
        for k in range(4):
            line = lines[k : k + 1]
            band = pltpu.roll(jnp.broadcast_to(line, (48, 256)), 0, 1, stride=1, stride_axis=0)
            tk[k, r * 48 : r * 48 + 48, :] = jnp.where(keep_rows, band, 0.0).astype(bf16)
    for k in range(4):
        tt[:, k * HALF : k * HALF + HALF] = tk[k].T
    tp[...] = jnp.zeros_like(tp)
    for r in range(4):
        tp[r, 0:45, :] = target[r].astype(f32)

    prow = iota((256, 16), 0)
    pcol = iota((256, 16), 1)
    third = lax.shift_right_logical(pcol * 11, 5)
    spot = third * 64 + (pcol - third * 3)
    put_right = jnp.where((pcol < 12) & (prow == spot + 45), 1.0, 0.0).astype(bf16)
    put_left = jnp.where((pcol < 12) & (prow == ((spot + 253) & 255)), 1.0, 0.0).astype(bf16)
    from_right.wait_recv()
    from_left.wait_recv()
    for m in range(2):
        halo = dot(put_right, halo_r[0, m]) + dot(put_left, halo_r[1, m])
        wide[m] = (wide[m].astype(f32) + halo).astype(bf16)

    for m in range(2):
        carry = None
        rows = slice(m * HALF, m * HALF + HALF)
        for k in range(4):
            value = dot(tk[k], wide[m])
            if k:
                value = pltpu.roll(value, k, 1)
            head = value[:, 0:128] if carry is None else value[:, 0:128] + carry
            spread[rows, 640 * k : 640 * k + 128] = head.astype(bf16)
            spread[rows, 640 * k + 128 : 640 * k + 640] = value[:, 128:640].astype(bf16)
            carry = value[:, 640:768]
        spread[rows, 2560:2688] = carry.astype(bf16)

    for load in loads:
        load.wait()
    conv = dot(spread[:, 0:WIDE], wd[...])
    hid[:, 0:CH] = (hs[:, 0:CH].astype(f32) + conv).astype(bf16)
    pre = dot(hid[:, 0:CH], we[...])
    inner = math.sqrt(2.0 / math.pi)
    square = pre * pre
    t = jnp.tanh(inner * (pre + 0.044715 * (square * pre)))
    act[:, 0:HID] = (0.5 * pre * (1.0 + t)).astype(bf16)
    gp[...] = 0.5 * (1.0 + t) + (0.5 * inner) * pre * (1.0 - t * t) * (
        1.0 + (3.0 * 0.044715) * square
    )
    mix[:, 0:CH] = (hid[:, 0:CH].astype(f32) + dot(act[:, 0:HID], wr[...])).astype(bf16)
    fields = dot(mix[:, 0:CH], wo[...])
    for p in range(8):
        block = jnp.concatenate(
            [fields[24 * p : 24 * p + 24], fields[HALF + 24 * p : HALF + 24 * p + 24]], axis=0
        )
        fs[p] = block.astype(bf16)
    there = []
    for d in range(1, 8):
        peer = lax.rem(me + d, 8)
        there.append(copies.send(fs.at[peer], fr.at[me], (peer, lon)))
    fr[me] = fs[me]

    spread_t[...] = spread[...].T
    hid_t[...] = hid[...].T
    act_t[...] = act[...].T
    mix_t[...] = mix[...].T

    for copy in there:
        copy.wait_recv()
    for p in range(8):
        block = fr[p].astype(f32)
        fv[2 * p] = block[0:24]
        fv[2 * p + 1] = block[24:48]
    slab, side = me // 2, lax.rem(me, 2)

    def slopes(i, carry):
        start = pl.multiple_of(i * 8, 8)
        rows = pl.ds(start, 8)
        goal = tp[slab, pl.ds(pl.multiple_of(side * 24 + start, 8), 8), :]
        for lanes in ((0, 128), (128, 128), (256, 32)):
            keep = iota((8, lanes[1]), 0) + (side * 24 + start) < 45
            pair_slopes(fv, og, goal, keep, lanes, rows)
        return carry

    lax.fori_loop(0, 3, slopes, 0)
    for p in range(8):
        gs[p] = jnp.concatenate([og[2 * p], og[2 * p + 1]], axis=0).astype(bf16)
    back = []
    for d in range(1, 8):
        peer = lax.rem(me + d, 8)
        back.append(copies.send(gs.at[peer], gr.at[me], (peer, lon)))
    gr[me] = gs[me]
    for copy in back:
        copy.wait_recv()
    blocks = [gr[p].astype(f32) for p in range(8)]
    fg[:, 0:OUTC] = jnp.concatenate(
        [b[0:24] for b in blocks] + [b[24:48] for b in blocks], axis=0
    ).astype(bf16)

    mixed_grad = dot_nt(fg[:, 0:OUTC], wo[...])
    mg[:, 0:CH] = mixed_grad.astype(bf16)
    pg[:, 0:HID] = (dot_nt(mg[:, 0:CH], wr[...]) * gp[...]).astype(bf16)
    hidden_grad = mg[:, 0:CH].astype(f32) + dot_nt(pg[:, 0:HID], we[...])
    hg[:, 0:CH] = hidden_grad.astype(bf16)

    def decode_part():
        value = dot(mix_t[0:656], fg[...])
        for j in range(3):
            grads[pl.ds(OFF_DECODE + j * U_DECODE, U_DECODE)] = flat_tiles(
                value[:, 128 * j : 128 * j + 128]
            )

    decode_part()
    grads[OFF_TAIL : OFF_TAIL + 177] = jnp.zeros((177, 16, 128), bf16)
    for c in range(3):
        value = dot(act_t[c * 432 : c * 432 + 432], mg[...])
        for j in range(5):
            grads[pl.ds(OFF_REDUCE + j * U_REDUCE + c * 27, 27)] = flat_tiles(
                value[:, 128 * j : 128 * j + 128]
            )
        grads[pl.ds(OFF_TAIL + c * 27, 27)] = flat_tiles(pltpu.roll(value[:, 640:768], 1, 1))
    value = dot(hid_t[0:656], pg[...])
    for j in range(10):
        grads[pl.ds(OFF_EXPAND + j * U_EXPAND, U_EXPAND)] = flat_tiles(
            value[:, 128 * j : 128 * j + 128]
        )
    tail = flat_tiles(pltpu.roll(value[:, 1280:1408], 2, 1))
    grads[pl.ds(OFF_TAIL, U_EXPAND)] = grads[pl.ds(OFF_TAIL, U_EXPAND)] + tail

    def disco_part(c, carry):
        value = dot(spread_t[pl.ds(pl.multiple_of(c * 368, 16), 368)], hg[...])
        for j in range(5):
            grads[pl.ds(OFF_DISCO + j * U_DISCO + c * 23, 23)] = flat_tiles(
                value[:, 128 * j : 128 * j + 128]
            )
        tail = flat_tiles(value[:, 640:768])
        spot = pl.ds(OFF_TAIL + c * 23, 23)
        grads[spot] = grads[spot] + tail
        return carry

    lax.fori_loop(0, 7, disco_part, 0)

    other = 1 - core
    waits = [
        copies.send(
            grads.at[pl.ds(other * 960 + p * PART, PART)], r0.at[pl.ds(p * PART, PART)], sibling
        )
        for p in range(3)
    ]

    for m in range(2):
        rows = slice(m * HALF, m * HALF + HALF)
        value = dot_nt(hg[rows, 0:CH], wd[...]).astype(bf16).astype(f32)
        value = jnp.concatenate([value, jnp.zeros((HALF, 124), f32)], axis=1)
        for k in range(4):
            piece = value[:, 640 * k : 640 * k + 768]
            if k:
                piece = pltpu.roll(piece, 768 - k, 1)
            sgs[k * HALF : k * HALF + HALF, :] = piece[:, 0:CH].astype(bf16)
        out = dot(tt[...], sgs[...])
        for s in range(4):
            ob[0, m, s] = out[((s + 3) % 4) * 64 + 56 : ((s + 3) % 4) * 64 + 64]
            ob[1, m, s] = out[s * 64 + 40 : s * 64 + 48]
            base = m * HALF + s * 48
            total = hg[base : base + 48, 0:CH].astype(f32) + out[s * 64 : s * 64 + 48]
            gp[base : base + 48, 0:CH] = total
    to_left = copies.send(ob.at[0], back_r.at[0], left)
    to_right = copies.send(ob.at[1], back_r.at[1], right)

    def add_tiles(dst, dst_at, parts, count, scale=None):
        step = 20 if count >= 20 else count

        def body(i, carry):
            total = None
            for ref, start in parts:
                piece = ref[pl.ds(start + i * step, step)].astype(f32)
                total = piece if total is None else total + piece
            if scale is not None:
                total = total * scale
            dst[pl.ds(dst_at + i * step, step)] = total.astype(bf16)
            return carry

        lax.fori_loop(0, count // step, body, 0)

    mine = [core * 960 + p * PART for p in range(3)]
    stage_a = []
    for p in range(3):
        waits[p].wait_recv()
        add_tiles(grads, mine[p], [(grads, mine[p]), (r0, p * PART)], PART)
        axis = AXES[p][0]
        for d in (1, 3, 2):
            there_at = moved(at, axis, d)
            stage_a.append(
                copies.send(
                    grads.at[pl.ds(mine[p] + there_at[axis] * 80, 80)],
                    r1.at[pl.ds((p * 3 + d - 1) * 80, 80)],
                    device(there_at),
                )
            )
    to_left.wait_recv()
    to_right.wait_recv()
    lane8 = iota((8, CH), 0)
    for m in range(2):
        for s in range(4):
            base = m * HALF + s * 48
            high = pltpu.roll(back_r[0, m, s], 5, 0)
            low = pltpu.roll(back_r[1, m, s], 3, 0)
            high = jnp.where((lane8 >= 2) & (lane8 < 5), high, 0.0)
            low = jnp.where(lane8 < 3, low, 0.0)
            gp[base : base + 8, 0:CH] = gp[base : base + 8, 0:CH] + low
            gp[base + 40 : base + 48, 0:CH] = gp[base + 40 : base + 48, 0:CH] + high
            lg[m, s] = gp[base : base + 48, 0:CH][0:45].astype(bf16)

    mine_a = [mine[p] + at[AXES[p][0]] * 80 for p in range(3)]
    mine_b = [mine_a[p] + at[AXES[p][1]] * 20 for p in range(3)]
    mine_c = [mine_b[p] + at[AXES[p][2]] * 5 for p in range(3)]
    stage_b = []
    for p in range(3):
        for copy in stage_a[3 * p : 3 * p + 3]:
            copy.wait_recv()
        add_tiles(
            grads,
            mine_a[p],
            [(grads, mine_a[p])] + [(r1, (p * 3 + d) * 80) for d in range(3)],
            80,
        )
        axis = AXES[p][1]
        for d in (1, 3, 2):
            there_at = moved(at, axis, d)
            stage_b.append(
                copies.send(
                    grads.at[pl.ds(mine_a[p] + there_at[axis] * 20, 20)],
                    r2.at[pl.ds((p * 3 + d - 1) * 20, 20)],
                    device(there_at),
                )
            )
    stage_c = []
    for p in range(3):
        for copy in stage_b[3 * p : 3 * p + 3]:
            copy.wait_recv()
        add_tiles(
            grads,
            mine_b[p],
            [(grads, mine_b[p])] + [(r2, (p * 3 + d) * 20) for d in range(3)],
            20,
        )
        axis = AXES[p][2]
        for d in (1, 3, 2):
            there_at = moved(at, axis, d)
            stage_c.append(
                copies.send(
                    grads.at[pl.ds(mine_b[p] + there_at[axis] * 5, 5)],
                    r3.at[pl.ds((p * 3 + d - 1) * 5, 5)],
                    device(there_at),
                )
            )
    factor = 1.0 / math.sqrt(46080.0)

    def spread_out(p, axis, start, count):
        region = flat.at[pl.ds(start, count)]
        return [
            copies.send(region, region, device(moved(at, axis, d))) for d in (1, 3, 2)
        ]

    gather_c = []
    for p in range(3):
        for copy in stage_c[3 * p : 3 * p + 3]:
            copy.wait_recv()
        add_tiles(
            flat,
            mine_c[p],
            [(grads, mine_c[p])] + [(r3, (p * 3 + d) * 5) for d in range(3)],
            5,
            factor,
        )
        gather_c.append(spread_out(p, AXES[p][2], mine_c[p], 5))
    gather_b = []
    for p in range(3):
        for copy in gather_c[p]:
            copy.wait_recv()
        gather_b.append(spread_out(p, AXES[p][1], mine_b[p], 20))
    gather_a = []
    for p in range(3):
        for copy in gather_b[p]:
            copy.wait_recv()
        gather_a.append(spread_out(p, AXES[p][0], mine_a[p], 80))
    last = []
    for p in range(3):
        region = flat.at[pl.ds(mine_a[p], 80)]
        last.append(copies.send(region, region, sibling))
    for p in range(3):
        axis = AXES[p][0]
        for d, copy in zip((1, 3, 2), gather_a[p]):
            copy.wait_recv()
            came = lax.rem(at[axis] + 4 - d, 4)
            region = flat.at[pl.ds(mine[p] + came * 80, 80)]
            last.append(copies.send(region, region, sibling))
    for copy in last:
        copy.wait_recv()
    copies.finish()


def unpack_kernel(flat, disco, expand, reduce, decode):
    def column(start, units):
        return flat[start : start + units].reshape(units * 16, 128)

    tail = column(OFF_TAIL, U_DISCO)
    for j in range(5):
        disco[:, 128 * j : 128 * j + 128] = column(OFF_DISCO + j * U_DISCO, U_DISCO)[0:WIDE]
        reduce[:, 128 * j : 128 * j + 128] = column(OFF_REDUCE + j * U_REDUCE, U_REDUCE)[0:HID]
    disco[:, 640:CH] = tail[0:WIDE, 0:1]
    wide_tail = tail.astype(f32)
    reduce[:, 640:CH] = pltpu.roll(wide_tail[0:1296], 127, 1)[0:HID, 0:1].astype(bf16)
    for j in range(10):
        expand[:, 128 * j : 128 * j + 128] = column(OFF_EXPAND + j * U_EXPAND, U_EXPAND)[0:CH]
    expand[:, 1280:HID] = pltpu.roll(wide_tail[0:656], 126, 1)[0:CH, 0:2].astype(bf16)
    for j in range(3):
        width = min(128, OUTC - 128 * j)
        piece = column(OFF_DECODE + j * U_DECODE, U_DECODE)[0:CH]
        decode[:, 128 * j : 128 * j + width] = piece[:, 0:width]


def per_device(
    latent,
    member_seeds,
    member_table,
    row_bands,
    disco_basis,
    w_disco,
    w_expand,
    w_reduce,
    w_decode,
    target,
):
    vm = pl.BlockSpec(memory_space=pltpu.VMEM)
    sm = pl.BlockSpec(memory_space=pltpu.SMEM)
    anywhere = pl.BlockSpec(memory_space=pl.ANY)
    V = pltpu.VMEM
    copies = 110
    scratch = [
        V((WIDE, CH), bf16),
        V((CH, HID), bf16),
        V((HID, CH), bf16),
        V((CH, OUTC), bf16),
        V((4, HALF, 256), bf16),
        V((256, 768), bf16),
        V((2, 256, 768), bf16),
        V((ROWS, 768), bf16),
        V((ROWS, 2688), bf16),
        V((2688, ROWS), bf16),
        V((ROWS, 768), bf16),
        V((768, ROWS), bf16),
        V((ROWS, HID), f32),
        V((ROWS, 1408), bf16),
        V((1408, ROWS), bf16),
        V((ROWS, 768), bf16),
        V((768, ROWS), bf16),
        V((2, 2, 16, 768), bf16),
        V((2, 2, 16, 768), bf16),
        V((8, 48, OUTC), bf16),
        V((8, 48, OUTC), bf16),
        V((16, 24, OUTC), f32),
        V((16, 24, OUTC), f32),
        V((8, 48, OUTC), bf16),
        V((8, 48, OUTC), bf16),
        V((4, 48, OUTC), f32),
        V((ROWS, 384), bf16),
        V((ROWS, 768), bf16),
        V((ROWS, 1408), bf16),
        V((ROWS, 768), bf16),
        V((768, CH), bf16),
        V((2, 2, 4, 8, CH), f32),
        V((2, 2, 4, 8, CH), f32),
        V((TILES, 16, 128), bf16),
        V((960, 16, 128), bf16),
        V((720, 16, 128), bf16),
        V((180, 16, 128), bf16),
        V((45, 16, 128), bf16),
        pltpu.SemaphoreType.DMA((copies,)),
        pltpu.SemaphoreType.DMA((copies,)),
        pltpu.SemaphoreType.DMA((4,)),
    ]
    lg, flat = pl.pallas_call(
        step_kernel,
        out_shape=(
            jax.ShapeDtypeStruct(latent.shape, bf16),
            jax.ShapeDtypeStruct((TILES, 16, 128), bf16),
        ),
        in_specs=[vm, sm, vm, sm, vm, anywhere, anywhere, anywhere, anywhere, vm],
        out_specs=(vm, vm),
        scratch_shapes=scratch,
        compiler_params=pltpu.CompilerParams(
            collective_id=0, has_side_effects=True, vmem_limit_bytes=66_000_000
        ),
        name="step",
    )(
        latent,
        member_seeds,
        member_table,
        row_bands,
        disco_basis,
        w_disco,
        w_expand,
        w_reduce,
        w_decode,
        target,
    )
    outs = pl.pallas_call(
        unpack_kernel,
        out_shape=(
            jax.ShapeDtypeStruct((WIDE, CH), bf16),
            jax.ShapeDtypeStruct((CH, HID), bf16),
            jax.ShapeDtypeStruct((HID, CH), bf16),
            jax.ShapeDtypeStruct((CH, OUTC), bf16),
        ),
        in_specs=[vm],
        out_specs=(vm, vm, vm, vm),
        compiler_params=pltpu.CompilerParams(vmem_limit_bytes=40_000_000),
        name="unpack",
    )(flat)
    return (lg,) + tuple(outs)


def solution(mesh):
    placed = (
        P("member", None, "lon", None),
        P("member"),
        P(),
        P(),
        P(),
        P(),
        P(),
        P(),
        P(),
        P(None, "lon", None),
    )
    return jax.shard_map(
        per_device,
        mesh=mesh,
        in_specs=placed,
        out_specs=(P("member", None, "lon", None), P(), P(), P(), P()),
        check_vma=False,
    )
```

```python
import functools
import math

import jax
import jax.numpy as jnp
from jax import lax
from jax.experimental import pallas as pl
from jax.experimental.pallas import tpu as pltpu
from jax.sharding import PartitionSpec as P

MESH = pl.DeviceIdType.MESH
f32 = jnp.float32
bf16 = jnp.bfloat16

CH = 641
HID = 1282
OUTC = 288
WIDE = 2564
ROWS = 384
HALF = 192
POINTS = 180
UNITS = 41
AXES = (("x", "y", "z"), ("y", "z", "x"), ("z", "x", "y"))
OFF_EXPAND, OFF_REDUCE, OFF_DECODE, OFF_DISCO, OFF_TAIL = 0, 410, 820, 960, 1780
U_DECODE = 18
TILES = 1824
WAVES = ((0, 160), (960, 144))


def place():
    member, lon = lax.axis_index("member"), lax.axis_index("lon")
    return {
        "x": (member % 2) * 2 + (lon // 2) % 2,
        "y": lon // 4,
        "z": member // 2,
        "c": lon % 2,
    }


def device(at):
    return (at["z"] * 2 + at["x"] // 2, at["y"] * 4 + (at["x"] % 2) * 2 + at["c"])


def moved(at, axis, step):
    there = dict(at)
    size = 2 if axis == "c" else 4
    there[axis] = lax.rem(at[axis] + step + size, size)
    return there


def iota(shape, dim):
    return lax.broadcasted_iota(jnp.int32, shape, dim)


def dot(a, b):
    return jnp.dot(a, b, preferred_element_type=f32)


def dot_nt(a, b):
    return lax.dot_general(a, b, (((1,), (1,)), ((), ())), preferred_element_type=f32)


def flat_tiles(value):
    return value.astype(bf16).reshape(value.shape[0] // 16, 16, 128)


class Copies:
    def __init__(self, send_sems, recv_sems):
        self.send_sems, self.recv_sems, self.count = send_sems, recv_sems, 0
        self.started = []

    def send(self, src, dst, to):
        copy = pltpu.make_async_remote_copy(
            src_ref=src,
            dst_ref=dst,
            send_sem=self.send_sems.at[self.count],
            recv_sem=self.recv_sems.at[self.count],
            device_id=to,
            device_id_type=MESH,
        )
        self.count += 1
        copy.start()
        self.started.append(copy)
        return copy

    def finish(self):
        for copy in self.started:
            copy.wait_send()


def pair_slopes(fv, og, tgt, me_h, lanes, rows):
    lo, width = lanes
    values = [fv[j, rows, lo : lo + width] for j in range(16)]
    sums = [None] * 16

    def slope(d):
        return d * lax.rsqrt(d * d + 0.25)

    for i in range(16):
        for j in range(i + 1, 16):
            s = slope(values[i] - values[j])
            sums[i] = s if sums[i] is None else sums[i] + s
            sums[j] = -s if sums[j] is None else sums[j] - s
    goal = tgt[:, lo : lo + width]
    keep = me_h
    for i in range(16):
        value = slope(values[i] - goal) - sums[i] * (1.0 / 15.0)
        og[i, rows, lo : lo + width] = jnp.where(keep, value, 0.0)


def step_kernel(
    latent,
    seeds,
    table,
    bands,
    basis,
    wd_any,
    we_any,
    wr_any,
    wo_any,
    target,
    lg,
    flat,
    wd,
    we,
    wr,
    wo,
    tk,
    tt,
    wide,
    hs,
    spread,
    hid,
    hid_t,
    gp,
    act,
    mix,
    halo_s,
    halo_r,
    fs,
    fr,
    fv,
    og,
    gs,
    gr,
    tp,
    fg,
    mg,
    pg,
    hg,
    sgs,
    ob,
    back_r,
    grads,
    r0,
    r1,
    r2,
    r3,
    send_sems,
    recv_sems,
    load_sems,
):
    at = place()
    me = lax.axis_index("member")
    lon = lax.axis_index("lon")
    left = (me, lax.rem(lon + 15, 16))
    right = (me, lax.rem(lon + 1, 16))
    core = at["c"]
    copies = Copies(send_sems, recv_sems)

    loads = []
    for i, (src, dst) in enumerate(((wd_any, wd), (we_any, we), (wr_any, wr), (wo_any, wo))):
        load = pltpu.make_async_copy(src, dst, load_sems.at[i])
        load.start()
        loads.append(load)

    sibling = device(moved(at, "c", 1))
    barrier = pltpu.get_barrier_semaphore()
    greet = [sibling, left, right]
    greet += [device(moved(at, axis, d)) for axis in "xyz" for d in (1, 2, 3)]
    greet += [(lax.rem(me + d, 8), lon) for d in range(1, 8)]
    for peer in greet:
        pl.semaphore_signal(barrier, inc=1, device_id=peer, device_id_type=MESH)

    for ref in (hid, mix, mg, hg):
        ref[:, 640:768] = jnp.zeros((ROWS, 128), bf16)
    for ref in (act, pg):
        ref[:, 1280:1408] = jnp.zeros((ROWS, 128), bf16)
    fg[:, 256:384] = jnp.zeros((ROWS, 128), bf16)
    low4 = iota((16, 768), 0) < 4
    for m in range(2):
        pick = jnp.where(iota((8, 64), 1) == seeds[m], 1.0, 0.0).astype(bf16)
        offset = dot(pick, table[...])[0:1]
        value = latent[m].astype(f32).reshape(POINTS, CH) + offset
        value = jnp.concatenate([value, jnp.zeros((POINTS, 127), f32)], axis=1)
        value = jnp.concatenate([value, jnp.zeros((76, 768), f32)], axis=0)
        seeded = value.astype(bf16)
        wide[m] = seeded
        hs[m * HALF : m * HALF + HALF] = seeded[0:HALF]
        first = pltpu.roll(value[0:16], 4, 0)
        final = pltpu.roll(value[160:192], 28, 0)[0:16]
        halo_s[0, m] = jnp.where(low4, 0.0, first).astype(bf16)
        halo_s[1, m] = jnp.where(low4, 0.0, final).astype(bf16)

    pl.semaphore_wait(barrier, len(greet))
    from_right = copies.send(halo_s.at[0], halo_r.at[0], left)
    from_left = copies.send(halo_s.at[1], halo_r.at[1], right)

    line = iota((8, 16), 0) & 3
    chosen = jnp.where(line == 0, bands[0], jnp.where(line == 1, bands[1], bands[2]))
    chosen = jnp.where(line == 3, bands[3], chosen)
    picks = jnp.where(iota((8, 16), 1) == chosen, 1.0, 0.0).astype(bf16)
    taps = dot_nt(picks, basis[...].astype(f32).reshape(196, 16).astype(bf16))
    line = iota((8, 196), 0) & 3
    index = iota((8, 196), 1)
    taps = jnp.where((index >= 28 * (3 - line)) & (index < 28 * (7 - line)), taps, 0.0)
    taps = taps.astype(bf16)
    index = iota((196, 256), 0)
    pair = lax.shift_right_logical(index, 2)
    a = lax.shift_right_logical(pair * 37, 8)
    spot = (4 * (pair - 7 * a) + a + (256 - 15)) & 255
    hit = iota((196, 256), 1) == spot
    sub = iota((8, 256), 0)
    for k in range(4):
        place_k = jnp.where(hit & ((index & 3) == k), 1.0, 0.0).astype(bf16)
        first = pltpu.roll(dot(taps, place_k), 0, 1, stride=1, stride_axis=0)
        lines = [first if i == 0 else pltpu.roll(first, 8 * i, 1) for i in range(23)]
        lines[22] = jnp.where(sub < 4, lines[22], 0.0)
        lines.append(jnp.zeros((8, 256), f32))
        band = jnp.concatenate(lines, axis=0).astype(bf16)
        tk[k] = band
        tt[:, k * HALF : k * HALF + HALF] = band.T
    tp[0:176] = target[0:44].astype(f32).reshape(176, OUTC)
    tp[176:184] = jnp.concatenate(
        [target[44].astype(f32), jnp.zeros((4, OUTC), f32)], axis=0
    )
    tp[184:192] = jnp.zeros((8, OUTC), f32)

    from_right.wait_recv()
    from_left.wait_recv()
    for m in range(2):
        wide[m, 176:192] = wide[m, 176:192] + halo_r[0, m]
        wide[m, 240:256] = halo_r[1, m]

    for m in range(2):
        carry = None
        rows = slice(m * HALF, m * HALF + HALF)
        for k in range(4):
            value = dot(tk[k], wide[m])
            if k:
                value = pltpu.roll(value, k, 1)
            head = value[:, 0:128] if carry is None else value[:, 0:128] + carry
            spread[rows, 640 * k : 640 * k + 128] = head.astype(bf16)
            spread[rows, 640 * k + 128 : 640 * k + 640] = value[:, 128:640].astype(bf16)
            carry = value[:, 640:768]
        spread[rows, 2560:2688] = carry.astype(bf16)

    for load in loads:
        load.wait()
    conv = dot_nt(spread[:, 0:WIDE], wd[...])
    hid[:, 0:CH] = (hs[:, 0:CH].astype(f32) + conv).astype(bf16)
    pre = dot(hid[:, 0:CH], we[...])
    inner = math.sqrt(2.0 / math.pi)
    square = pre * pre
    t = jnp.tanh(inner * (pre + 0.044715 * (square * pre)))
    act[:, 0:HID] = (0.5 * pre * (1.0 + t)).astype(bf16)
    gp[...] = 0.5 * (1.0 + t) + (0.5 * inner) * pre * (1.0 - t * t) * (
        1.0 + (3.0 * 0.044715) * square
    )
    mix[:, 0:CH] = (hid[:, 0:CH].astype(f32) + dot_nt(act[:, 0:HID], wr[...])).astype(bf16)
    fields = dot_nt(mix[:, 0:CH], wo[...])
    for p in range(8):
        block = jnp.concatenate(
            [fields[24 * p : 24 * p + 24], fields[HALF + 24 * p : HALF + 24 * p + 24]], axis=0
        )
        fs[p] = block.astype(bf16)
    there = []
    for d in range(1, 8):
        peer = lax.rem(me + d, 8)
        there.append(copies.send(fs.at[peer], fr.at[me], (peer, lon)))
    fr[me] = fs[me]
    hid_t[...] = hid[...].T

    for copy in there:
        copy.wait_recv()
    for p in range(8):
        block = fr[p].astype(f32)
        fv[2 * p] = block[0:24]
        fv[2 * p + 1] = block[24:48]

    def slopes(i, carry):
        start = pl.multiple_of(i * 8, 8)
        rows = pl.ds(start, 8)
        goal = tp[pl.ds(pl.multiple_of(me * 24 + start, 8), 8), :]
        for lanes in ((0, 128), (128, 128), (256, 32)):
            keep = iota((8, lanes[1]), 0) + (me * 24 + start) < POINTS
            pair_slopes(fv, og, goal, keep, lanes, rows)
        return carry

    lax.fori_loop(0, 3, slopes, 0)
    for p in range(8):
        gs[p] = jnp.concatenate([og[2 * p], og[2 * p + 1]], axis=0).astype(bf16)
    back = []
    for d in range(1, 8):
        peer = lax.rem(me + d, 8)
        back.append(copies.send(gs.at[peer], gr.at[me], (peer, lon)))
    gr[me] = gs[me]
    for copy in back:
        copy.wait_recv()
    blocks = [gr[p].astype(f32) for p in range(8)]
    fg[:, 0:OUTC] = jnp.concatenate(
        [b[0:24] for b in blocks] + [b[24:48] for b in blocks], axis=0
    ).astype(bf16)

    factor = 1.0 / math.sqrt(46080.0)

    def add_tiles(dst, dst_at, parts, count, step, scale=None):
        def body(i, carry):
            total = None
            for ref, start in parts:
                piece = ref[pl.ds(start + i * step, step)].astype(f32)
                total = piece if total is None else total + piece
            if scale is not None:
                total = total * scale
            dst[pl.ds(dst_at + i * step, step)] = total.astype(bf16)
            return carry

        lax.fori_loop(0, count // step, body, 0)

    def reduced(wave, p):
        base, size = WAVES[wave]
        sa, sb = size // 4, size // 16
        start = base + 2 * p * size
        mine = start + core * size
        first, second, third = AXES[p]
        mine_a = mine + at[first] * sa
        mine_b = mine_a + at[second] * sb
        lane = (0 if wave == 0 else 480) + p * size
        r0_at = lane
        lane_a = (0 if wave == 0 else 360) + p * 3 * sa
        lane_b = (0 if wave == 0 else 90) + p * 3 * sb
        lane_c = (0 if wave == 0 else 120) + p * 4 * sb

        def to_peers(axis, src, dst):
            return [
                copies.send(src(d, moved(at, axis, d)), dst(d), device(moved(at, axis, d)))
                for d in (1, 3, 2)
            ]

        across = copies.send(
            grads.at[pl.ds(start + (1 - core) * size, size)],
            r0.at[pl.ds(r0_at, size)],
            sibling,
        )
        yield
        across.wait_recv()
        add_tiles(grads, mine, [(grads, mine), (r0, r0_at)], size, 16)
        sent = to_peers(
            first,
            lambda d, to: grads.at[pl.ds(mine + to[first] * sa, sa)],
            lambda d: r1.at[pl.ds(lane_a + (d - 1) * sa, sa)],
        )
        yield
        for copy in sent:
            copy.wait_recv()
        add_tiles(
            grads, mine_a, [(grads, mine_a)] + [(r1, lane_a + d * sa) for d in range(3)], sa, sb
        )
        sent = to_peers(
            second,
            lambda d, to: grads.at[pl.ds(mine_a + to[second] * sb, sb)],
            lambda d: r2.at[pl.ds(lane_b + (d - 1) * sb, sb)],
        )
        yield
        for copy in sent:
            copy.wait_recv()
        add_tiles(
            grads, mine_b, [(grads, mine_b)] + [(r2, lane_b + d * sb) for d in range(3)], sb, sb
        )
        own = pl.ds(lane_c + at[third] * sb, sb)
        sent = to_peers(
            third, lambda d, to: grads.at[pl.ds(mine_b, sb)], lambda d: r3.at[own]
        )
        r3[own] = grads[pl.ds(mine_b, sb)]
        yield
        for copy in sent:
            copy.wait_recv()
        add_tiles(flat, mine_b, [(r3, lane_c + q * sb) for q in range(4)], sb, sb, factor)
        region_b = flat.at[pl.ds(mine_b, sb)]
        sent = to_peers(second, lambda d, to: region_b, lambda d: region_b)
        yield
        for copy in sent:
            copy.wait_recv()
        region_a = flat.at[pl.ds(mine_a, sa)]
        sent = to_peers(first, lambda d, to: region_a, lambda d: region_a)
        last = [copies.send(region_a, region_a, sibling)]
        yield
        for d, copy in zip((1, 3, 2), sent):
            copy.wait_recv()
            came = lax.rem(at[first] + 4 - d, 4)
            region = flat.at[pl.ds(mine + came * sa, sa)]
            last.append(copies.send(region, region, sibling))
        yield
        for copy in last:
            copy.wait_recv()
        yield

    one = [reduced(0, p) for p in range(3)]
    two = [reduced(1, p) for p in range(3)]

    def advance(wave):
        for part in wave:
            next(part)

    def put_columns(value, off, units, count):
        for j in range(count):
            grads[pl.ds(off + j * units, units)] = flat_tiles(
                value[0 : units * 16, 128 * j : 128 * j + 128]
            )

    mixed_grad = dot(fg[:, 0:OUTC], wo[...])
    mg[:, 0:CH] = mixed_grad.astype(bf16)
    pg[:, 0:HID] = (dot(mg[:, 0:CH], wr[...]) * gp[...]).astype(bf16)

    value = dot(hid_t[0:656], pg[...])
    put_columns(value, OFF_EXPAND, UNITS, 10)
    tail = pltpu.roll(value[:, 1280:1408], 4, 1)
    value = dot(mg[...].T[0:656], act[...])
    put_columns(value, OFF_REDUCE, UNITS, 10)
    tail = tail + pltpu.roll(value[:, 1280:1408], 6, 1)
    value = dot(fg[...].T[0:OUTC], mix[...])
    put_columns(value, OFF_DECODE, U_DECODE, 5)
    last_lane = jnp.concatenate([value[:, 640:768], jnp.zeros((656 - OUTC, 128), f32)], axis=0)
    tail = tail + pltpu.roll(last_lane, 8, 1)
    advance(one)

    hidden_grad = mg[:, 0:CH].astype(f32) + dot_nt(pg[:, 0:HID], we[...])
    hg[:, 0:CH] = hidden_grad.astype(bf16)
    hg_t = hg[...].T[0:656]
    for c in range(5):
        value = dot(hg_t, spread[:, 512 * c : 512 * c + 512])
        put_columns(value, OFF_DISCO + 4 * c * UNITS, UNITS, 4)
        if c == 1:
            advance(one)
    tail = tail + dot(hg_t, spread[:, 2560:2688])
    put_columns(tail, OFF_TAIL, UNITS, 1)
    advance(two)

    for m in range(2):
        rows = slice(m * HALF, m * HALF + HALF)
        value = dot(hg[rows, 0:CH], wd[...]).astype(bf16).astype(f32)
        value = jnp.concatenate([value, jnp.zeros((HALF, 124), f32)], axis=1)
        for k in range(4):
            piece = value[:, 640 * k : 640 * k + 768]
            if k:
                piece = pltpu.roll(piece, 768 - k, 1)
            sgs[k * HALF : k * HALF + HALF, :] = piece[:, 0:CH].astype(bf16)
        if m == 0:
            advance(two)
        out = dot(tt[...], sgs[...])
        ob[0, m] = out[240:256]
        ob[1, m] = out[176:192]
        gp[rows, 0:CH] = hg[rows, 0:CH].astype(f32) + out[0:HALF]
    to_left = copies.send(ob.at[0], back_r.at[0], left)
    to_right = copies.send(ob.at[1], back_r.at[1], right)
    advance(one)
    advance(one)
    to_left.wait_recv()
    to_right.wait_recv()
    low = iota((16, CH), 0)
    for m in range(2):
        base = m * HALF
        after = pltpu.roll(back_r[1, m], 12, 0)
        gp[base : base + 16, 0:CH] = gp[base : base + 16, 0:CH] + jnp.where(low < 12, after, 0.0)
        before = jnp.where(low >= 4, back_r[0, m], 0.0)
        before = jnp.concatenate([before, jnp.zeros((16, CH), f32)], axis=0)
        before = pltpu.roll(before, 4, 0)
        spot = slice(base + 160, base + 192)
        gp[spot, 0:CH] = gp[spot, 0:CH] + before
        total = gp[base : base + HALF, 0:CH]
        lg[m] = total[0:POINTS].reshape(45, 4, CH).astype(bf16)
    advance(two)
    advance(one)
    advance(two)
    advance(one)
    advance(two)
    advance(one)
    advance(two)
    advance(two)
    advance(one)
    advance(two)
    copies.finish()


def unpack_kernel(flat, disco, expand, reduce, decode):
    def column(start, units):
        return flat[start : start + units].reshape(units * 16, 128)

    tail = column(OFF_TAIL, UNITS)
    wide_tail = tail.astype(f32)
    for j in range(20):
        disco[:, 128 * j : 128 * j + 128] = column(OFF_DISCO + j * UNITS, UNITS)[0:CH]
    disco[:, 2560:WIDE] = tail[0:CH, 0:4]
    for j in range(10):
        expand[:, 128 * j : 128 * j + 128] = column(OFF_EXPAND + j * UNITS, UNITS)[0:CH]
        reduce[:, 128 * j : 128 * j + 128] = column(OFF_REDUCE + j * UNITS, UNITS)[0:CH]
    expand[:, 1280:HID] = pltpu.roll(wide_tail, 124, 1)[0:CH, 0:2].astype(bf16)
    reduce[:, 1280:HID] = pltpu.roll(wide_tail, 122, 1)[0:CH, 0:2].astype(bf16)
    for j in range(5):
        decode[:, 128 * j : 128 * j + 128] = column(OFF_DECODE + j * U_DECODE, U_DECODE)
    decode[:, 640:CH] = pltpu.roll(wide_tail, 120, 1)[0:OUTC, 0:1].astype(bf16)


def per_device(
    latent,
    member_seeds,
    member_table,
    row_bands,
    disco_basis,
    w_disco,
    w_expand,
    w_reduce,
    w_decode,
    target,
):
    vm = pl.BlockSpec(memory_space=pltpu.VMEM)
    sm = pl.BlockSpec(memory_space=pltpu.SMEM)
    anywhere = pl.BlockSpec(memory_space=pl.ANY)
    V = pltpu.VMEM
    copies = 150
    scratch = [
        V((CH, WIDE), bf16),
        V((CH, HID), bf16),
        V((CH, HID), bf16),
        V((OUTC, CH), bf16),
        V((4, HALF, 256), bf16),
        V((256, 768), bf16),
        V((2, 256, 768), bf16),
        V((ROWS, 768), bf16),
        V((ROWS, 2688), bf16),
        V((ROWS, 768), bf16),
        V((768, ROWS), bf16),
        V((ROWS, HID), f32),
        V((ROWS, 1408), bf16),
        V((ROWS, 768), bf16),
        V((2, 2, 16, 768), bf16),
        V((2, 2, 16, 768), bf16),
        V((8, 48, OUTC), bf16),
        V((8, 48, OUTC), bf16),
        V((16, 24, OUTC), f32),
        V((16, 24, OUTC), f32),
        V((8, 48, OUTC), bf16),
        V((8, 48, OUTC), bf16),
        V((HALF, OUTC), f32),
        V((ROWS, 384), bf16),
        V((ROWS, 768), bf16),
        V((ROWS, 1408), bf16),
        V((ROWS, 768), bf16),
        V((768, CH), bf16),
        V((2, 2, 16, CH), f32),
        V((2, 2, 16, CH), f32),
        V((TILES, 16, 128), bf16),
        V((912, 16, 128), bf16),
        V((684, 16, 128), bf16),
        V((171, 16, 128), bf16),
        V((228, 16, 128), bf16),
        pltpu.SemaphoreType.DMA((copies,)),
        pltpu.SemaphoreType.DMA((copies,)),
        pltpu.SemaphoreType.DMA((4,)),
    ]
    lg, flat = pl.pallas_call(
        step_kernel,
        out_shape=(
            jax.ShapeDtypeStruct((2, 45, 4, CH), bf16),
            jax.ShapeDtypeStruct((TILES, 16, 128), bf16),
        ),
        in_specs=[vm, sm, vm, sm, vm, anywhere, anywhere, anywhere, anywhere, vm],
        out_specs=(vm, vm),
        scratch_shapes=scratch,
        compiler_params=pltpu.CompilerParams(
            collective_id=0, has_side_effects=True, vmem_limit_bytes=54_000_000
        ),
        name="step",
    )(
        latent.transpose(0, 2, 1, 3),
        member_seeds,
        member_table,
        row_bands,
        disco_basis.transpose(2, 3, 1, 0),
        w_disco.T,
        w_expand,
        w_reduce.T,
        w_decode.T,
        target.transpose(1, 0, 2),
    )
    disco, expand, reduce, decode = pl.pallas_call(
        unpack_kernel,
        out_shape=(
            jax.ShapeDtypeStruct((CH, WIDE), bf16),
            jax.ShapeDtypeStruct((CH, HID), bf16),
            jax.ShapeDtypeStruct((CH, HID), bf16),
            jax.ShapeDtypeStruct((OUTC, CH), bf16),
        ),
        in_specs=[vm],
        out_specs=(vm, vm, vm, vm),
        compiler_params=pltpu.CompilerParams(vmem_limit_bytes=30_000_000),
        name="unpack",
    )(flat)
    return (lg.transpose(0, 2, 1, 3), disco.T, expand, reduce.T, decode.T)


def solution(mesh):
    placed = (
        P("member", None, "lon", None),
        P("member"),
        P(),
        P(),
        P(),
        P(),
        P(),
        P(),
        P(),
        P(None, "lon", None),
    )
    return jax.shard_map(
        per_device,
        mesh=mesh,
        in_specs=placed,
        out_specs=(P("member", None, "lon", None), P(), P(), P(), P()),
        check_vma=False,
    )
```

```python
import functools
import math

import jax
import jax.numpy as jnp
from jax import lax
from jax.experimental import pallas as pl
from jax.experimental.pallas import tpu as pltpu
from jax.sharding import PartitionSpec as P

MESH = pl.DeviceIdType.MESH
f32 = jnp.float32
bf16 = jnp.bfloat16

CH = 641
HID = 1282
OUTC = 288
WIDE = 2564
ROWS = 384
HALF = 192
POINTS = 180
UNITS = 41
AXES = (("x", "y", "z"), ("y", "z", "x"), ("z", "x", "y"))
OFF_EXPAND, OFF_REDUCE, OFF_DECODE, OFF_DISCO, OFF_TAIL = 0, 410, 820, 960, 1780
U_DECODE = 18
TILES = 1824
WAVES = ((0, 160), (960, 144))


def place():
    member, lon = lax.axis_index("member"), lax.axis_index("lon")
    return {
        "x": (member % 2) * 2 + (lon // 2) % 2,
        "y": lon // 4,
        "z": member // 2,
        "c": lon % 2,
    }


def device(at):
    return (at["z"] * 2 + at["x"] // 2, at["y"] * 4 + (at["x"] % 2) * 2 + at["c"])


def moved(at, axis, step):
    there = dict(at)
    size = 2 if axis == "c" else 4
    there[axis] = lax.rem(at[axis] + step + size, size)
    return there


def iota(shape, dim):
    return lax.broadcasted_iota(jnp.int32, shape, dim)


def dot(a, b):
    return jnp.dot(a, b, preferred_element_type=f32)


def dot_nt(a, b):
    return lax.dot_general(a, b, (((1,), (1,)), ((), ())), preferred_element_type=f32)


def flat_tiles(value):
    return value.astype(bf16).reshape(value.shape[0] // 16, 16, 128)


class Copies:
    def __init__(self, send_sems, recv_sems):
        self.send_sems, self.recv_sems, self.count = send_sems, recv_sems, 0
        self.started = []

    def send(self, src, dst, to):
        copy = pltpu.make_async_remote_copy(
            src_ref=src,
            dst_ref=dst,
            send_sem=self.send_sems.at[self.count],
            recv_sem=self.recv_sems.at[self.count],
            device_id=to,
            device_id_type=MESH,
        )
        self.count += 1
        copy.start()
        self.started.append(copy)
        return copy

    def finish(self):
        for copy in self.started:
            copy.wait_send()


def pair_slopes(fv, og, tgt, me_h, lanes, rows):
    lo, width = lanes
    values = [fv[j, rows, lo : lo + width] for j in range(16)]
    sums = [None] * 16

    def slope(d):
        return d * lax.rsqrt(d * d + 0.25)

    for i in range(16):
        for j in range(i + 1, 16):
            s = slope(values[i] - values[j])
            sums[i] = s if sums[i] is None else sums[i] + s
            sums[j] = -s if sums[j] is None else sums[j] - s
    goal = tgt[:, lo : lo + width]
    keep = me_h
    for i in range(16):
        value = slope(values[i] - goal) - sums[i] * (1.0 / 15.0)
        og[i, rows, lo : lo + width] = jnp.where(keep, value, 0.0)


def step_kernel(
    latent_any,
    seeds_any,
    table_any,
    bands_any,
    basis_any,
    wd_any,
    we_any,
    wr_any,
    wo_any,
    target_any,
    lg,
    flat_any,
    flat,
    latent,
    seeds,
    table,
    bands,
    basis,
    target,
    wd,
    we,
    wr,
    wo,
    tk,
    tt,
    wide,
    hs,
    spread,
    hid,
    hid_t,
    gp,
    act,
    mix,
    halo_s,
    halo_r,
    fs,
    fr,
    fv,
    og,
    gs,
    gr,
    tp,
    fg,
    mg,
    pg,
    hg,
    sgs,
    ob,
    back_r,
    grads,
    r0,
    r1,
    r2,
    r3,
    send_sems,
    recv_sems,
    load_sems,
    store_sems,
):
    at = place()
    me = lax.axis_index("member")
    lon = lax.axis_index("lon")
    left = (me, lax.rem(lon + 15, 16))
    right = (me, lax.rem(lon + 1, 16))
    core = at["c"]
    copies = Copies(send_sems, recv_sems)

    early = []
    for i, (src, dst) in enumerate(
        (
            (latent_any, latent),
            (seeds_any, seeds),
            (table_any, table),
            (bands_any, bands),
            (basis_any, basis),
            (target_any, target),
        )
    ):
        load = pltpu.make_async_copy(src, dst, load_sems.at[4 + i])
        load.start()
        early.append(load)
    loads = []
    for i, (src, dst) in enumerate(((wd_any, wd), (we_any, we), (wr_any, wr), (wo_any, wo))):
        load = pltpu.make_async_copy(src, dst, load_sems.at[i])
        load.start()
        loads.append(load)

    sibling = device(moved(at, "c", 1))
    barrier = pltpu.get_barrier_semaphore()
    greet = [sibling, left, right]
    greet += [device(moved(at, axis, d)) for axis in "xyz" for d in (1, 2, 3)]
    greet += [(lax.rem(me + d, 8), lon) for d in range(1, 8)]
    for peer in greet:
        pl.semaphore_signal(barrier, inc=1, device_id=peer, device_id_type=MESH)

    for ref in (hid, mix, mg, hg):
        ref[:, 640:768] = jnp.zeros((ROWS, 128), bf16)
    for ref in (act, pg):
        ref[:, 1280:1408] = jnp.zeros((ROWS, 128), bf16)
    fg[:, 256:384] = jnp.zeros((ROWS, 128), bf16)
    low4 = iota((16, 768), 0) < 4
    for load in early:
        load.wait()
    for m in range(2):
        pick = jnp.where(iota((8, 64), 1) == seeds[m], 1.0, 0.0).astype(bf16)
        offset = dot(pick, table[...])[0:1]
        value = latent[m].astype(f32).reshape(POINTS, CH) + offset
        value = jnp.concatenate([value, jnp.zeros((POINTS, 127), f32)], axis=1)
        value = jnp.concatenate([value, jnp.zeros((76, 768), f32)], axis=0)
        seeded = value.astype(bf16)
        wide[m] = seeded
        hs[m * HALF : m * HALF + HALF] = seeded[0:HALF]
        first = pltpu.roll(value[0:16], 4, 0)
        final = pltpu.roll(value[160:192], 28, 0)[0:16]
        halo_s[0, m] = jnp.where(low4, 0.0, first).astype(bf16)
        halo_s[1, m] = jnp.where(low4, 0.0, final).astype(bf16)

    pl.semaphore_wait(barrier, len(greet))
    from_right = copies.send(halo_s.at[0], halo_r.at[0], left)
    from_left = copies.send(halo_s.at[1], halo_r.at[1], right)

    line = iota((8, 16), 0) & 3
    chosen = jnp.where(line == 0, bands[0], jnp.where(line == 1, bands[1], bands[2]))
    chosen = jnp.where(line == 3, bands[3], chosen)
    picks = jnp.where(iota((8, 16), 1) == chosen, 1.0, 0.0).astype(bf16)
    taps = dot_nt(picks, basis[...].astype(f32).reshape(196, 16).astype(bf16))
    line = iota((8, 196), 0) & 3
    index = iota((8, 196), 1)
    taps = jnp.where((index >= 28 * (3 - line)) & (index < 28 * (7 - line)), taps, 0.0)
    taps = taps.astype(bf16)
    index = iota((196, 256), 0)
    pair = lax.shift_right_logical(index, 2)
    a = lax.shift_right_logical(pair * 37, 8)
    spot = (4 * (pair - 7 * a) + a + (256 - 15)) & 255
    hit = iota((196, 256), 1) == spot
    sub = iota((8, 256), 0)
    for k in range(4):
        place_k = jnp.where(hit & ((index & 3) == k), 1.0, 0.0).astype(bf16)
        first = pltpu.roll(dot(taps, place_k), 0, 1, stride=1, stride_axis=0)
        lines = [first if i == 0 else pltpu.roll(first, 8 * i, 1) for i in range(23)]
        lines[22] = jnp.where(sub < 4, lines[22], 0.0)
        lines.append(jnp.zeros((8, 256), f32))
        band = jnp.concatenate(lines, axis=0).astype(bf16)
        tk[k] = band
        tt[:, k * HALF : k * HALF + HALF] = band.T
    tp[0:176] = target[0:44].astype(f32).reshape(176, OUTC)
    tp[176:184] = jnp.concatenate(
        [target[44].astype(f32), jnp.zeros((4, OUTC), f32)], axis=0
    )
    tp[184:192] = jnp.zeros((8, OUTC), f32)

    from_right.wait_recv()
    from_left.wait_recv()
    for m in range(2):
        wide[m, 176:192] = wide[m, 176:192] + halo_r[0, m]
        wide[m, 240:256] = halo_r[1, m]

    for m in range(2):
        carry = None
        rows = slice(m * HALF, m * HALF + HALF)
        for k in range(4):
            value = dot(tk[k], wide[m])
            if k:
                value = pltpu.roll(value, k, 1)
            head = value[:, 0:128] if carry is None else value[:, 0:128] + carry
            spread[rows, 640 * k : 640 * k + 128] = head.astype(bf16)
            spread[rows, 640 * k + 128 : 640 * k + 640] = value[:, 128:640].astype(bf16)
            carry = value[:, 640:768]
        spread[rows, 2560:2688] = carry.astype(bf16)

    for load in loads:
        load.wait()
    conv = dot_nt(spread[:, 0:WIDE], wd[...])
    hid[:, 0:CH] = (hs[:, 0:CH].astype(f32) + conv).astype(bf16)
    pre = dot(hid[:, 0:CH], we[...])
    inner = math.sqrt(2.0 / math.pi)
    square = pre * pre
    t = jnp.tanh(inner * (pre + 0.044715 * (square * pre)))
    act[:, 0:HID] = (0.5 * pre * (1.0 + t)).astype(bf16)
    gp[...] = 0.5 * (1.0 + t) + (0.5 * inner) * pre * (1.0 - t * t) * (
        1.0 + (3.0 * 0.044715) * square
    )
    mix[:, 0:CH] = (hid[:, 0:CH].astype(f32) + dot_nt(act[:, 0:HID], wr[...])).astype(bf16)
    fields = dot_nt(mix[:, 0:CH], wo[...])
    for p in range(8):
        block = jnp.concatenate(
            [fields[24 * p : 24 * p + 24], fields[HALF + 24 * p : HALF + 24 * p + 24]], axis=0
        )
        fs[p] = block.astype(bf16)
    there = []
    for d in range(1, 8):
        peer = lax.rem(me + d, 8)
        there.append(copies.send(fs.at[peer], fr.at[me], (peer, lon)))
    fr[me] = fs[me]
    hid_t[...] = hid[...].T

    for copy in there:
        copy.wait_recv()
    for p in range(8):
        block = fr[p].astype(f32)
        fv[2 * p] = block[0:24]
        fv[2 * p + 1] = block[24:48]

    def slopes(i, carry):
        start = pl.multiple_of(i * 8, 8)
        rows = pl.ds(start, 8)
        goal = tp[pl.ds(pl.multiple_of(me * 24 + start, 8), 8), :]
        for lanes in ((0, 128), (128, 128), (256, 32)):
            keep = iota((8, lanes[1]), 0) + (me * 24 + start) < POINTS
            pair_slopes(fv, og, goal, keep, lanes, rows)
        return carry

    lax.fori_loop(0, 3, slopes, 0)
    for p in range(8):
        gs[p] = jnp.concatenate([og[2 * p], og[2 * p + 1]], axis=0).astype(bf16)
    back = []
    for d in range(1, 8):
        peer = lax.rem(me + d, 8)
        back.append(copies.send(gs.at[peer], gr.at[me], (peer, lon)))
    gr[me] = gs[me]
    for copy in back:
        copy.wait_recv()
    blocks = [gr[p].astype(f32) for p in range(8)]
    fg[:, 0:OUTC] = jnp.concatenate(
        [b[0:24] for b in blocks] + [b[24:48] for b in blocks], axis=0
    ).astype(bf16)

    factor = 1.0 / math.sqrt(46080.0)
    stores = []

    def store(start, count):
        spot = pl.ds(start, count)
        copy = pltpu.make_async_copy(flat.at[spot], flat_any.at[spot], store_sems.at[len(stores)])
        copy.start()
        stores.append(copy)

    def add_tiles(dst, dst_at, parts, count, step, scale=None):
        def body(i, carry):
            total = None
            for ref, start in parts:
                piece = ref[pl.ds(start + i * step, step)].astype(f32)
                total = piece if total is None else total + piece
            if scale is not None:
                total = total * scale
            dst[pl.ds(dst_at + i * step, step)] = total.astype(bf16)
            return carry

        lax.fori_loop(0, count // step, body, 0)

    def reduced(wave, p):
        base, size = WAVES[wave]
        sa, sb = size // 4, size // 16
        start = base + 2 * p * size
        mine = start + core * size
        first, second, third = AXES[p]
        mine_a = mine + at[first] * sa
        mine_b = mine_a + at[second] * sb
        lane = (0 if wave == 0 else 480) + p * size
        r0_at = lane
        lane_a = (0 if wave == 0 else 360) + p * 3 * sa
        lane_b = (0 if wave == 0 else 90) + p * 3 * sb
        lane_c = (0 if wave == 0 else 120) + p * 4 * sb

        def to_peers(axis, src, dst):
            return [
                copies.send(src(d, moved(at, axis, d)), dst(d), device(moved(at, axis, d)))
                for d in (1, 3, 2)
            ]

        half = sa // 2
        onward, backward = device(moved(at, first, 1)), device(moved(at, first, 3))

        def block(step, side):
            return mine + lax.rem(at[first] + step, 4) * sa + side * half

        def landing(step):
            return lane_a + step * half

        across = copies.send(
            grads.at[pl.ds(start + (1 - core) * size, size)],
            r0.at[pl.ds(r0_at, size)],
            sibling,
        )
        yield
        across.wait_recv()
        add_tiles(grads, mine, [(grads, mine), (r0, r0_at)], size, 16)

        def give(at_tile, step, to):
            return copies.send(grads.at[pl.ds(at_tile, half)], r1.at[pl.ds(landing(step), half)], to)

        relay_on = give(block(2, 0), 4, onward)
        relay_back = give(block(2, 1), 5, backward)
        sent = [give(block(1, 1), 1, onward), give(block(3, 0), 2, backward)]
        yield
        relay_on.wait_recv()
        add_tiles(grads, block(1, 0), [(grads, block(1, 0)), (r1, landing(4))], half, half)
        sent.append(give(block(1, 0), 0, onward))
        relay_back.wait_recv()
        add_tiles(grads, block(3, 1), [(grads, block(3, 1)), (r1, landing(5))], half, half)
        sent.append(give(block(3, 1), 3, backward))
        yield
        for copy in sent:
            copy.wait_recv()
        add_tiles(
            grads, mine_a, [(grads, mine_a)] + [(r1, lane_a + d * sa) for d in range(2)], sa, sb
        )
        sent = to_peers(
            second,
            lambda d, to: grads.at[pl.ds(mine_a + to[second] * sb, sb)],
            lambda d: r2.at[pl.ds(lane_b + (d - 1) * sb, sb)],
        )
        yield
        for copy in sent:
            copy.wait_recv()
        add_tiles(
            grads, mine_b, [(grads, mine_b)] + [(r2, lane_b + d * sb) for d in range(3)], sb, sb
        )
        own = pl.ds(lane_c + at[third] * sb, sb)
        sent = to_peers(
            third, lambda d, to: grads.at[pl.ds(mine_b, sb)], lambda d: r3.at[own]
        )
        r3[own] = grads[pl.ds(mine_b, sb)]
        yield
        for copy in sent:
            copy.wait_recv()
        add_tiles(flat, mine_b, [(r3, lane_c + q * sb) for q in range(4)], sb, sb, factor)
        region_b = flat.at[pl.ds(mine_b, sb)]
        sent = to_peers(second, lambda d, to: region_b, lambda d: region_b)
        yield
        for copy in sent:
            copy.wait_recv()

        def pass_on(step, side, to):
            region = flat.at[pl.ds(block(step, side), half)]
            return copies.send(region, region, to)

        def share(step):
            region = flat.at[pl.ds(block(step, 0), sa)]
            copy = copies.send(region, region, sibling)
            store(block(step, 0), sa)
            return copy

        from_before = pass_on(0, 0, onward)
        from_after = pass_on(0, 1, backward)
        rest_before = pass_on(0, 1, onward)
        rest_after = pass_on(0, 0, backward)
        last = [share(0)]
        yield
        from_before.wait_recv()
        far_before = pass_on(3, 0, onward)
        from_after.wait_recv()
        far_after = pass_on(1, 1, backward)
        yield
        rest_before.wait_recv()
        last.append(share(3))
        rest_after.wait_recv()
        last.append(share(1))
        yield
        far_before.wait_recv()
        far_after.wait_recv()
        last.append(share(2))
        yield
        for step, copy in zip((0, 3, 1, 2), last):
            copy.wait_recv()
            store(block(step, 0) + (1 - 2 * core) * size, sa)
        yield

    one = [reduced(0, p) for p in range(3)]
    two = [reduced(1, p) for p in range(3)]

    def advance(wave):
        for part in wave:
            next(part)

    def put_columns(value, off, units, count):
        for j in range(count):
            grads[pl.ds(off + j * units, units)] = flat_tiles(
                value[0 : units * 16, 128 * j : 128 * j + 128]
            )

    mixed_grad = dot(fg[:, 0:OUTC], wo[...])
    mg[:, 0:CH] = mixed_grad.astype(bf16)
    pg[:, 0:HID] = (dot(mg[:, 0:CH], wr[...]) * gp[...]).astype(bf16)

    value = dot(hid_t[0:656], pg[...])
    put_columns(value, OFF_EXPAND, UNITS, 10)
    tail = pltpu.roll(value[:, 1280:1408], 4, 1)
    value = dot(mg[...].T[0:656], act[...])
    put_columns(value, OFF_REDUCE, UNITS, 10)
    tail = tail + pltpu.roll(value[:, 1280:1408], 6, 1)
    value = dot(fg[...].T[0:OUTC], mix[...])
    put_columns(value, OFF_DECODE, U_DECODE, 5)
    last_lane = jnp.concatenate([value[:, 640:768], jnp.zeros((656 - OUTC, 128), f32)], axis=0)
    tail = tail + pltpu.roll(last_lane, 8, 1)
    advance(one)

    hidden_grad = mg[:, 0:CH].astype(f32) + dot_nt(pg[:, 0:HID], we[...])
    hg[:, 0:CH] = hidden_grad.astype(bf16)
    hg_t = hg[...].T[0:656]
    for c in range(5):
        value = dot(hg_t, spread[:, 512 * c : 512 * c + 512])
        put_columns(value, OFF_DISCO + 4 * c * UNITS, UNITS, 4)
        if c == 1:
            advance(one)
    tail = tail + dot(hg_t, spread[:, 2560:2688])
    put_columns(tail, OFF_TAIL, UNITS, 1)
    advance(two)

    for m in range(2):
        rows = slice(m * HALF, m * HALF + HALF)
        value = dot(hg[rows, 0:CH], wd[...]).astype(bf16).astype(f32)
        value = jnp.concatenate([value, jnp.zeros((HALF, 124), f32)], axis=1)
        for k in range(4):
            piece = value[:, 640 * k : 640 * k + 768]
            if k:
                piece = pltpu.roll(piece, 768 - k, 1)
            sgs[k * HALF : k * HALF + HALF, :] = piece[:, 0:CH].astype(bf16)
        if m == 0:
            advance(two)
            advance(one)
        out = dot(tt[...], sgs[...])
        ob[0, m] = out[240:256]
        ob[1, m] = out[176:192]
        gp[rows, 0:CH] = hg[rows, 0:CH].astype(f32) + out[0:HALF]
    to_left = copies.send(ob.at[0], back_r.at[0], left)
    to_right = copies.send(ob.at[1], back_r.at[1], right)
    advance(two)
    advance(one)
    to_left.wait_recv()
    to_right.wait_recv()
    low = iota((16, CH), 0)
    for m in range(2):
        base = m * HALF
        after = pltpu.roll(back_r[1, m], 12, 0)
        gp[base : base + 16, 0:CH] = gp[base : base + 16, 0:CH] + jnp.where(low < 12, after, 0.0)
        before = jnp.where(low >= 4, back_r[0, m], 0.0)
        before = jnp.concatenate([before, jnp.zeros((16, CH), f32)], axis=0)
        before = pltpu.roll(before, 4, 0)
        spot = slice(base + 160, base + 192)
        gp[spot, 0:CH] = gp[spot, 0:CH] + before
        total = gp[base : base + HALF, 0:CH]
        lg[m] = total[0:POINTS].reshape(45, 4, CH).astype(bf16)
    advance(two)
    for _ in range(7):
        advance(one)
        advance(two)
    for copy in stores:
        copy.wait()
    copies.finish()


def unpack_kernel(
    flat_any,
    lg_any,
    disco_any,
    expand_any,
    reduce_any,
    decode_any,
    lg_out,
    flat,
    disco,
    expand,
    reduce,
    decode,
    lg,
    in_sems,
    out_sems,
):
    pieces = [(OFF_TAIL, UNITS), (OFF_EXPAND, 410), (OFF_REDUCE, 410), (OFF_DECODE, 90)]
    pieces += [(OFF_DISCO + 205 * q, 205) for q in range(4)]
    loads = []
    for i, (start, count) in enumerate(pieces):
        spot = pl.ds(start, count)
        loads.append(pltpu.make_async_copy(flat_any.at[spot], flat.at[spot], in_sems.at[i]))
        loads[-1].start()
    loads.append(pltpu.make_async_copy(lg_any, lg, in_sems.at[8]))
    loads[-1].start()
    stores = []

    def store(src, dst):
        stores.append(pltpu.make_async_copy(src, dst, out_sems.at[len(stores)]))
        stores[-1].start()

    def column(start, units):
        return flat[start : start + units].reshape(units * 16, 128)

    loads[0].wait()
    tail = column(OFF_TAIL, UNITS)
    wide_tail = tail.astype(f32)
    loads[1].wait()
    for j in range(10):
        expand[:, 128 * j : 128 * j + 128] = column(OFF_EXPAND + j * UNITS, UNITS)[0:CH]
    expand[:, 1280:HID] = pltpu.roll(wide_tail, 124, 1)[0:CH, 0:2].astype(bf16)
    store(expand, expand_any)
    loads[2].wait()
    for j in range(10):
        reduce[:, 128 * j : 128 * j + 128] = column(OFF_REDUCE + j * UNITS, UNITS)[0:CH]
    reduce[:, 1280:HID] = pltpu.roll(wide_tail, 122, 1)[0:CH, 0:2].astype(bf16)
    store(reduce, reduce_any)
    loads[3].wait()
    for j in range(5):
        decode[:, 128 * j : 128 * j + 128] = column(OFF_DECODE + j * U_DECODE, U_DECODE)
    decode[:, 640:CH] = pltpu.roll(wide_tail, 120, 1)[0:OUTC, 0:1].astype(bf16)
    store(decode, decode_any)
    disco[:, 2560:WIDE] = tail[0:CH, 0:4]
    for q in range(4):
        loads[4 + q].wait()
        for j in range(5 * q, 5 * q + 5):
            disco[:, 128 * j : 128 * j + 128] = column(OFF_DISCO + j * UNITS, UNITS)[0:CH]
        spot = slice(640 * q, WIDE if q == 3 else 640 * q + 640)
        store(disco.at[:, spot], disco_any.at[:, spot])
    loads[8].wait()
    store(lg, lg_out)
    for copy in stores:
        copy.wait()


def per_device(
    latent,
    member_seeds,
    member_table,
    row_bands,
    disco_basis,
    w_disco,
    w_expand,
    w_reduce,
    w_decode,
    target,
):
    vm = pl.BlockSpec(memory_space=pltpu.VMEM)
    hbm = pl.BlockSpec(memory_space=pltpu.HBM)
    V = pltpu.VMEM
    copies = 180
    scratch = [
        V((TILES, 16, 128), bf16),
        V((2, 45, 4, CH), bf16),
        pltpu.SMEM((2,), jnp.int32),
        V((64, CH), bf16),
        pltpu.SMEM((4,), jnp.int32),
        V((7, 7, 4, 16), bf16),
        V((45, 4, OUTC), bf16),
        V((CH, WIDE), bf16),
        V((CH, HID), bf16),
        V((CH, HID), bf16),
        V((OUTC, CH), bf16),
        V((4, HALF, 256), bf16),
        V((256, 768), bf16),
        V((2, 256, 768), bf16),
        V((ROWS, 768), bf16),
        V((ROWS, 2688), bf16),
        V((ROWS, 768), bf16),
        V((768, ROWS), bf16),
        V((ROWS, HID), f32),
        V((ROWS, 1408), bf16),
        V((ROWS, 768), bf16),
        V((2, 2, 16, 768), bf16),
        V((2, 2, 16, 768), bf16),
        V((8, 48, OUTC), bf16),
        V((8, 48, OUTC), bf16),
        V((16, 24, OUTC), f32),
        V((16, 24, OUTC), f32),
        V((8, 48, OUTC), bf16),
        V((8, 48, OUTC), bf16),
        V((HALF, OUTC), f32),
        V((ROWS, 384), bf16),
        V((ROWS, 768), bf16),
        V((ROWS, 1408), bf16),
        V((ROWS, 768), bf16),
        V((768, CH), bf16),
        V((2, 2, 16, CH), f32),
        V((2, 2, 16, CH), f32),
        V((TILES, 16, 128), bf16),
        V((912, 16, 128), bf16),
        V((684, 16, 128), bf16),
        V((171, 16, 128), bf16),
        V((228, 16, 128), bf16),
        pltpu.SemaphoreType.DMA((copies,)),
        pltpu.SemaphoreType.DMA((copies,)),
        pltpu.SemaphoreType.DMA((10,)),
        pltpu.SemaphoreType.DMA((48,)),
    ]
    lg, flat = pl.pallas_call(
        step_kernel,
        out_shape=(
            jax.ShapeDtypeStruct((2, 45, 4, CH), bf16),
            jax.ShapeDtypeStruct((TILES, 16, 128), bf16),
        ),
        in_specs=[hbm] * 10,
        out_specs=(vm, hbm),
        scratch_shapes=scratch,
        compiler_params=pltpu.CompilerParams(
            collective_id=0, has_side_effects=True, vmem_limit_bytes=67_000_000
        ),
        name="step",
    )(
        latent.transpose(0, 2, 1, 3),
        member_seeds,
        member_table,
        row_bands,
        disco_basis.transpose(2, 3, 1, 0),
        w_disco.T,
        w_expand,
        w_reduce.T,
        w_decode.T,
        target.transpose(1, 0, 2),
    )
    shapes = ((CH, WIDE), (CH, HID), (CH, HID), (OUTC, CH), (2, 45, 4, CH))
    disco, expand, reduce, decode, lg = pl.pallas_call(
        unpack_kernel,
        out_shape=tuple(jax.ShapeDtypeStruct(shape, bf16) for shape in shapes),
        in_specs=[hbm, hbm],
        out_specs=(hbm,) * 5,
        scratch_shapes=[V((TILES, 16, 128), bf16)]
        + [V(shape, bf16) for shape in shapes]
        + [pltpu.SemaphoreType.DMA((9,)), pltpu.SemaphoreType.DMA((8,))],
        compiler_params=pltpu.CompilerParams(vmem_limit_bytes=67_000_000),
        name="unpack",
    )(flat, lg)
    return (lg.transpose(0, 2, 1, 3), disco.T, expand, reduce.T, decode.T)


def solution(mesh):
    placed = (
        P("member", None, "lon", None),
        P("member"),
        P(),
        P(),
        P(),
        P(),
        P(),
        P(),
        P(),
        P(None, "lon", None),
    )
    return jax.shard_map(
        per_device,
        mesh=mesh,
        in_specs=placed,
        out_specs=(P("member", None, "lon", None), P(), P(), P(), P()),
        check_vma=False,
    )
```

```python
import functools
import math

import jax
import jax.numpy as jnp
from jax import lax
from jax.experimental import pallas as pl
from jax.experimental.pallas import tpu as pltpu
from jax.sharding import PartitionSpec as P

MESH = pl.DeviceIdType.MESH
f32 = jnp.float32
bf16 = jnp.bfloat16

CH = 641
HID = 1282
OUTC = 288
WIDE = 2564
ROWS = 384
HALF = 192
POINTS = 180
UNITS = 41
AXES = (("x", "y", "z"), ("y", "z", "x"), ("z", "x", "y"))
OFF_EXPAND, OFF_REDUCE, OFF_DECODE, OFF_DISCO, OFF_TAIL = 0, 410, 820, 960, 1780
U_DECODE = 18
TILES = 1824
WAVES = ((0, 160), (960, 144))


def place():
    member, lon = lax.axis_index("member"), lax.axis_index("lon")
    return {
        "x": (member % 2) * 2 + (lon // 2) % 2,
        "y": lon // 4,
        "z": member // 2,
        "c": lon % 2,
    }


def device(at):
    return (at["z"] * 2 + at["x"] // 2, at["y"] * 4 + (at["x"] % 2) * 2 + at["c"])


def moved(at, axis, step):
    there = dict(at)
    size = 2 if axis == "c" else 4
    there[axis] = lax.rem(at[axis] + step + size, size)
    return there


def iota(shape, dim):
    return lax.broadcasted_iota(jnp.int32, shape, dim)


def dot(a, b):
    return jnp.dot(a, b, preferred_element_type=f32)


def dot_nt(a, b):
    return lax.dot_general(a, b, (((1,), (1,)), ((), ())), preferred_element_type=f32)


def flat_tiles(value):
    return value.astype(bf16).reshape(value.shape[0] // 16, 16, 128)


class Copies:
    def __init__(self, send_sems, recv_sems):
        self.send_sems, self.recv_sems, self.count = send_sems, recv_sems, 0
        self.started = []

    def send(self, src, dst, to):
        copy = pltpu.make_async_remote_copy(
            src_ref=src,
            dst_ref=dst,
            send_sem=self.send_sems.at[self.count],
            recv_sem=self.recv_sems.at[self.count],
            device_id=to,
            device_id_type=MESH,
        )
        self.count += 1
        copy.start()
        self.started.append(copy)
        return copy

    def finish(self):
        for copy in self.started:
            copy.wait_send()


def pair_slopes(fv, og, tgt, me_h, lanes, rows):
    lo, width = lanes
    values = [fv[j, rows, lo : lo + width] for j in range(16)]
    sums = [None] * 16

    def slope(d):
        return d * lax.rsqrt(d * d + 0.25)

    for i in range(16):
        for j in range(i + 1, 16):
            s = slope(values[i] - values[j])
            sums[i] = s if sums[i] is None else sums[i] + s
            sums[j] = -s if sums[j] is None else sums[j] - s
    goal = tgt[:, lo : lo + width]
    keep = me_h
    for i in range(16):
        value = slope(values[i] - goal) - sums[i] * (1.0 / 15.0)
        og[i, rows, lo : lo + width] = jnp.where(keep, value, 0.0)


def step_kernel(
    latent_any,
    seeds_any,
    table_any,
    bands_any,
    basis_any,
    wd_any,
    we_any,
    wr_any,
    wo_any,
    target_any,
    lg,
    flat,
    latent,
    seeds,
    table,
    bands,
    basis,
    target,
    wd,
    we,
    wr,
    wo,
    tk,
    tt,
    wide,
    hs,
    spread,
    hid,
    hid_t,
    gp,
    act,
    mix,
    halo_s,
    halo_r,
    fs,
    fr,
    fv,
    og,
    gs,
    gr,
    tp,
    fg,
    mg,
    pg,
    hg,
    sgs,
    ob,
    back_r,
    grads,
    r0,
    r1,
    r2,
    r3,
    send_sems,
    recv_sems,
    load_sems,
):
    at = place()
    me = lax.axis_index("member")
    lon = lax.axis_index("lon")
    left = (me, lax.rem(lon + 15, 16))
    right = (me, lax.rem(lon + 1, 16))
    core = at["c"]
    copies = Copies(send_sems, recv_sems)

    early = []
    for i, (src, dst) in enumerate(
        (
            (latent_any, latent),
            (seeds_any, seeds),
            (table_any, table),
            (bands_any, bands),
            (basis_any, basis),
            (target_any, target),
        )
    ):
        load = pltpu.make_async_copy(src, dst, load_sems.at[4 + i])
        load.start()
        early.append(load)
    loads = []
    for i, (src, dst) in enumerate(((wd_any, wd), (we_any, we), (wr_any, wr), (wo_any, wo))):
        load = pltpu.make_async_copy(src, dst, load_sems.at[i])
        load.start()
        loads.append(load)

    sibling = device(moved(at, "c", 1))
    barrier = pltpu.get_barrier_semaphore()
    greet = [sibling, left, right]
    greet += [device(moved(at, axis, d)) for axis in "xyz" for d in (1, 2, 3)]
    greet += [(lax.rem(me + d, 8), lon) for d in range(1, 8)]
    for peer in greet:
        pl.semaphore_signal(barrier, inc=1, device_id=peer, device_id_type=MESH)

    for ref in (hid, mix, mg, hg):
        ref[:, 640:768] = jnp.zeros((ROWS, 128), bf16)
    for ref in (act, pg):
        ref[:, 1280:1408] = jnp.zeros((ROWS, 128), bf16)
    fg[:, 256:384] = jnp.zeros((ROWS, 128), bf16)
    low4 = iota((16, 768), 0) < 4
    for load in early:
        load.wait()
    for m in range(2):
        pick = jnp.where(iota((8, 64), 1) == seeds[m], 1.0, 0.0).astype(bf16)
        offset = dot(pick, table[...])[0:1]
        value = latent[m].astype(f32).reshape(POINTS, CH) + offset
        value = jnp.concatenate([value, jnp.zeros((POINTS, 127), f32)], axis=1)
        value = jnp.concatenate([value, jnp.zeros((76, 768), f32)], axis=0)
        seeded = value.astype(bf16)
        wide[m] = seeded
        hs[m * HALF : m * HALF + HALF] = seeded[0:HALF]
        first = pltpu.roll(value[0:16], 4, 0)
        final = pltpu.roll(value[160:192], 28, 0)[0:16]
        halo_s[0, m] = jnp.where(low4, 0.0, first).astype(bf16)
        halo_s[1, m] = jnp.where(low4, 0.0, final).astype(bf16)

    pl.semaphore_wait(barrier, len(greet))
    from_right = copies.send(halo_s.at[0], halo_r.at[0], left)
    from_left = copies.send(halo_s.at[1], halo_r.at[1], right)

    line = iota((8, 16), 0) & 3
    chosen = jnp.where(line == 0, bands[0], jnp.where(line == 1, bands[1], bands[2]))
    chosen = jnp.where(line == 3, bands[3], chosen)
    picks = jnp.where(iota((8, 16), 1) == chosen, 1.0, 0.0).astype(bf16)
    taps = dot_nt(picks, basis[...].astype(f32).reshape(196, 16).astype(bf16))
    line = iota((8, 196), 0) & 3
    index = iota((8, 196), 1)
    taps = jnp.where((index >= 28 * (3 - line)) & (index < 28 * (7 - line)), taps, 0.0)
    taps = taps.astype(bf16)
    index = iota((196, 256), 0)
    pair = lax.shift_right_logical(index, 2)
    a = lax.shift_right_logical(pair * 37, 8)
    spot = (4 * (pair - 7 * a) + a + (256 - 15)) & 255
    hit = iota((196, 256), 1) == spot
    sub = iota((8, 256), 0)
    for k in range(4):
        place_k = jnp.where(hit & ((index & 3) == k), 1.0, 0.0).astype(bf16)
        first = pltpu.roll(dot(taps, place_k), 0, 1, stride=1, stride_axis=0)
        lines = [first if i == 0 else pltpu.roll(first, 8 * i, 1) for i in range(23)]
        lines[22] = jnp.where(sub < 4, lines[22], 0.0)
        lines.append(jnp.zeros((8, 256), f32))
        band = jnp.concatenate(lines, axis=0).astype(bf16)
        tk[k] = band
        tt[:, k * HALF : k * HALF + HALF] = band.T
    tp[0:176] = target[0:44].astype(f32).reshape(176, OUTC)
    tp[176:184] = jnp.concatenate(
        [target[44].astype(f32), jnp.zeros((4, OUTC), f32)], axis=0
    )
    tp[184:192] = jnp.zeros((8, OUTC), f32)

    from_right.wait_recv()
    from_left.wait_recv()
    for m in range(2):
        wide[m, 176:192] = wide[m, 176:192] + halo_r[0, m]
        wide[m, 240:256] = halo_r[1, m]

    for m in range(2):
        carry = None
        rows = slice(m * HALF, m * HALF + HALF)
        for k in range(4):
            value = dot(tk[k], wide[m])
            if k:
                value = pltpu.roll(value, k, 1)
            head = value[:, 0:128] if carry is None else value[:, 0:128] + carry
            spread[rows, 640 * k : 640 * k + 128] = head.astype(bf16)
            spread[rows, 640 * k + 128 : 640 * k + 640] = value[:, 128:640].astype(bf16)
            carry = value[:, 640:768]
        spread[rows, 2560:2688] = carry.astype(bf16)

    for load in loads:
        load.wait()
    conv = dot_nt(spread[:, 0:WIDE], wd[...])
    hid[:, 0:CH] = (hs[:, 0:CH].astype(f32) + conv).astype(bf16)
    pre = dot(hid[:, 0:CH], we[...])
    inner = math.sqrt(2.0 / math.pi)
    square = pre * pre
    t = jnp.tanh(inner * (pre + 0.044715 * (square * pre)))
    act[:, 0:HID] = (0.5 * pre * (1.0 + t)).astype(bf16)
    gp[...] = 0.5 * (1.0 + t) + (0.5 * inner) * pre * (1.0 - t * t) * (
        1.0 + (3.0 * 0.044715) * square
    )
    mix[:, 0:CH] = (hid[:, 0:CH].astype(f32) + dot_nt(act[:, 0:HID], wr[...])).astype(bf16)
    fields = dot_nt(mix[:, 0:CH], wo[...])
    for p in range(8):
        block = jnp.concatenate(
            [fields[24 * p : 24 * p + 24], fields[HALF + 24 * p : HALF + 24 * p + 24]], axis=0
        )
        fs[p] = block.astype(bf16)
    there = []
    for d in range(1, 8):
        peer = lax.rem(me + d, 8)
        there.append(copies.send(fs.at[peer], fr.at[me], (peer, lon)))
    fr[me] = fs[me]
    hid_t[...] = hid[...].T

    for copy in there:
        copy.wait_recv()
    for p in range(8):
        block = fr[p].astype(f32)
        fv[2 * p] = block[0:24]
        fv[2 * p + 1] = block[24:48]

    def slopes(i, carry):
        start = pl.multiple_of(i * 8, 8)
        rows = pl.ds(start, 8)
        goal = tp[pl.ds(pl.multiple_of(me * 24 + start, 8), 8), :]
        for lanes in ((0, 128), (128, 128), (256, 32)):
            keep = iota((8, lanes[1]), 0) + (me * 24 + start) < POINTS
            pair_slopes(fv, og, goal, keep, lanes, rows)
        return carry

    lax.fori_loop(0, 3, slopes, 0)
    for p in range(8):
        gs[p] = jnp.concatenate([og[2 * p], og[2 * p + 1]], axis=0).astype(bf16)
    back = []
    for d in range(1, 8):
        peer = lax.rem(me + d, 8)
        back.append(copies.send(gs.at[peer], gr.at[me], (peer, lon)))
    gr[me] = gs[me]
    for copy in back:
        copy.wait_recv()
    blocks = [gr[p].astype(f32) for p in range(8)]
    fg[:, 0:OUTC] = jnp.concatenate(
        [b[0:24] for b in blocks] + [b[24:48] for b in blocks], axis=0
    ).astype(bf16)

    factor = 1.0 / math.sqrt(46080.0)
    def add_tiles(dst, dst_at, parts, count, step, scale=None):
        def body(i, carry):
            total = None
            for ref, start in parts:
                piece = ref[pl.ds(start + i * step, step)].astype(f32)
                total = piece if total is None else total + piece
            if scale is not None:
                total = total * scale
            dst[pl.ds(dst_at + i * step, step)] = total.astype(bf16)
            return carry

        lax.fori_loop(0, count // step, body, 0)

    def reduced(wave, p):
        base, size = WAVES[wave]
        sa, sb = size // 4, size // 16
        start = base + 2 * p * size
        mine = start + core * size
        first, second, third = AXES[p]
        mine_a = mine + at[first] * sa
        mine_b = mine_a + at[second] * sb
        lane = (0 if wave == 0 else 480) + p * size
        r0_at = lane
        lane_a = (0 if wave == 0 else 360) + p * 3 * sa
        lane_b = (0 if wave == 0 else 90) + p * 3 * sb
        lane_c = (0 if wave == 0 else 120) + p * 4 * sb

        def to_peers(axis, src, dst):
            return [
                copies.send(src(d, moved(at, axis, d)), dst(d), device(moved(at, axis, d)))
                for d in (1, 3, 2)
            ]

        half = sa // 2
        onward, backward = device(moved(at, first, 1)), device(moved(at, first, 3))

        def block(step, side):
            return mine + lax.rem(at[first] + step, 4) * sa + side * half

        def landing(step):
            return lane_a + step * half

        across = copies.send(
            grads.at[pl.ds(start + (1 - core) * size, size)],
            r0.at[pl.ds(r0_at, size)],
            sibling,
        )
        yield
        across.wait_recv()
        add_tiles(grads, mine, [(grads, mine), (r0, r0_at)], size, 16)

        def give(at_tile, step, to):
            return copies.send(grads.at[pl.ds(at_tile, half)], r1.at[pl.ds(landing(step), half)], to)

        relay_on = give(block(2, 0), 4, onward)
        relay_back = give(block(2, 1), 5, backward)
        sent = [give(block(1, 1), 1, onward), give(block(3, 0), 2, backward)]
        yield
        relay_on.wait_recv()
        add_tiles(grads, block(1, 0), [(grads, block(1, 0)), (r1, landing(4))], half, half)
        sent.append(give(block(1, 0), 0, onward))
        relay_back.wait_recv()
        add_tiles(grads, block(3, 1), [(grads, block(3, 1)), (r1, landing(5))], half, half)
        sent.append(give(block(3, 1), 3, backward))
        yield
        for copy in sent:
            copy.wait_recv()
        add_tiles(
            grads, mine_a, [(grads, mine_a)] + [(r1, lane_a + d * sa) for d in range(2)], sa, sb
        )
        sent = to_peers(
            second,
            lambda d, to: grads.at[pl.ds(mine_a + to[second] * sb, sb)],
            lambda d: r2.at[pl.ds(lane_b + (d - 1) * sb, sb)],
        )
        yield
        for copy in sent:
            copy.wait_recv()
        add_tiles(
            grads, mine_b, [(grads, mine_b)] + [(r2, lane_b + d * sb) for d in range(3)], sb, sb
        )
        own = pl.ds(lane_c + at[third] * sb, sb)
        sent = to_peers(
            third, lambda d, to: grads.at[pl.ds(mine_b, sb)], lambda d: r3.at[own]
        )
        r3[own] = grads[pl.ds(mine_b, sb)]
        yield
        for copy in sent:
            copy.wait_recv()
        add_tiles(flat, mine_b, [(r3, lane_c + q * sb) for q in range(4)], sb, sb, factor)
        region_b = flat.at[pl.ds(mine_b, sb)]
        sent = to_peers(second, lambda d, to: region_b, lambda d: region_b)
        yield
        for copy in sent:
            copy.wait_recv()

        def pass_on(step, side, to):
            region = flat.at[pl.ds(block(step, side), half)]
            return copies.send(region, region, to)

        def share(step):
            region = flat.at[pl.ds(block(step, 0), sa)]
            return copies.send(region, region, sibling)

        from_before = pass_on(0, 0, onward)
        from_after = pass_on(0, 1, backward)
        rest_before = pass_on(0, 1, onward)
        rest_after = pass_on(0, 0, backward)
        last = [share(0)]
        yield
        from_before.wait_recv()
        far_before = pass_on(3, 0, onward)
        from_after.wait_recv()
        far_after = pass_on(1, 1, backward)
        yield
        rest_before.wait_recv()
        last.append(share(3))
        rest_after.wait_recv()
        last.append(share(1))
        yield
        far_before.wait_recv()
        far_after.wait_recv()
        last.append(share(2))
        yield
        for copy in last:
            copy.wait_recv()
        yield

    one = [reduced(0, p) for p in range(3)]
    two = [reduced(1, p) for p in range(3)]

    def advance(*parts):
        for part in parts:
            next(part)

    def put_columns(value, off, units, count):
        for j in range(count):
            grads[pl.ds(off + j * units, units)] = flat_tiles(
                value[0 : units * 16, 128 * j : 128 * j + 128]
            )

    mixed_grad = dot(fg[:, 0:OUTC], wo[...])
    mg[:, 0:CH] = mixed_grad.astype(bf16)
    pg[:, 0:HID] = (dot(mg[:, 0:CH], wr[...]) * gp[...]).astype(bf16)

    value = dot(hid_t[0:656], pg[...])
    put_columns(value, OFF_EXPAND, UNITS, 10)
    advance(one[0])
    tail = pltpu.roll(value[:, 1280:1408], 4, 1)
    value = dot(mg[...].T[0:656], act[...])
    put_columns(value, OFF_REDUCE, UNITS, 10)
    advance(one[1], one[0])
    tail = tail + pltpu.roll(value[:, 1280:1408], 6, 1)
    value = dot(fg[...].T[0:OUTC], mix[...])
    put_columns(value, OFF_DECODE, U_DECODE, 5)
    last_lane = jnp.concatenate([value[:, 640:768], jnp.zeros((656 - OUTC, 128), f32)], axis=0)
    tail = tail + pltpu.roll(last_lane, 8, 1)
    advance(one[2], one[1])

    hidden_grad = mg[:, 0:CH].astype(f32) + dot_nt(pg[:, 0:HID], we[...])
    hg[:, 0:CH] = hidden_grad.astype(bf16)
    advance(one[2])
    hg_t = hg[...].T[0:656]
    for c in range(5):
        value = dot(hg_t, spread[:, 512 * c : 512 * c + 512])
        put_columns(value, OFF_DISCO + 4 * c * UNITS, UNITS, 4)
        if c == 1:
            advance(two[0], one[0])
        if c == 3:
            advance(two[1], two[0], one[1])
    tail = tail + dot(hg_t, spread[:, 2560:2688])
    put_columns(tail, OFF_TAIL, UNITS, 1)
    advance(two[2], two[1], one[2])

    for m in range(2):
        rows = slice(m * HALF, m * HALF + HALF)
        value = dot(hg[rows, 0:CH], wd[...]).astype(bf16).astype(f32)
        value = jnp.concatenate([value, jnp.zeros((HALF, 124), f32)], axis=1)
        for k in range(4):
            piece = value[:, 640 * k : 640 * k + 768]
            if k:
                piece = pltpu.roll(piece, 768 - k, 1)
            sgs[k * HALF : k * HALF + HALF, :] = piece[:, 0:CH].astype(bf16)
        advance(two[2] if m == 0 else two[0])
        out = dot(tt[...], sgs[...])
        ob[0, m] = out[240:256]
        ob[1, m] = out[176:192]
        gp[rows, 0:CH] = hg[rows, 0:CH].astype(f32) + out[0:HALF]
        if m == 0:
            advance(one[0])
    to_left = copies.send(ob.at[0], back_r.at[0], left)
    to_right = copies.send(ob.at[1], back_r.at[1], right)
    advance(one[1], two[1], one[2], two[2], one[0])
    to_left.wait_recv()
    to_right.wait_recv()
    low = iota((16, CH), 0)
    for m in range(2):
        base = m * HALF
        after = pltpu.roll(back_r[1, m], 12, 0)
        gp[base : base + 16, 0:CH] = gp[base : base + 16, 0:CH] + jnp.where(low < 12, after, 0.0)
        before = jnp.where(low >= 4, back_r[0, m], 0.0)
        before = jnp.concatenate([before, jnp.zeros((16, CH), f32)], axis=0)
        before = pltpu.roll(before, 4, 0)
        spot = slice(base + 160, base + 192)
        gp[spot, 0:CH] = gp[spot, 0:CH] + before
        total = gp[base : base + HALF, 0:CH]
        lg[m] = total[0:POINTS].reshape(45, 4, CH).astype(bf16)
    advance(one[1], one[2])
    for _ in range(6):
        advance(*two)
        advance(*one)
    advance(*two)
    advance(*two)
    copies.finish()


def unpack_kernel(
    flat,
    lg,
    disco_any,
    expand_any,
    reduce_any,
    decode_any,
    lg_out,
    disco,
    expand,
    reduce,
    decode,
    out_sems,
):
    stores = []

    def store(src, dst):
        stores.append(pltpu.make_async_copy(src, dst, out_sems.at[len(stores)]))
        stores[-1].start()

    store(lg, lg_out)

    def column(start, units):
        return flat[start : start + units].reshape(units * 16, 128)

    tail = column(OFF_TAIL, UNITS)
    wide_tail = tail.astype(f32)
    for j in range(10):
        expand[:, 128 * j : 128 * j + 128] = column(OFF_EXPAND + j * UNITS, UNITS)[0:CH]
    expand[:, 1280:HID] = pltpu.roll(wide_tail, 124, 1)[0:CH, 0:2].astype(bf16)
    store(expand, expand_any)
    for j in range(10):
        reduce[:, 128 * j : 128 * j + 128] = column(OFF_REDUCE + j * UNITS, UNITS)[0:CH]
    reduce[:, 1280:HID] = pltpu.roll(wide_tail, 122, 1)[0:CH, 0:2].astype(bf16)
    store(reduce, reduce_any)
    for j in range(5):
        decode[:, 128 * j : 128 * j + 128] = column(OFF_DECODE + j * U_DECODE, U_DECODE)
    decode[:, 640:CH] = pltpu.roll(wide_tail, 120, 1)[0:OUTC, 0:1].astype(bf16)
    store(decode, decode_any)
    disco[:, 2560:WIDE] = tail[0:CH, 0:4]
    for q in range(4):
        for j in range(5 * q, 5 * q + 5):
            disco[:, 128 * j : 128 * j + 128] = column(OFF_DISCO + j * UNITS, UNITS)[0:CH]
        spot = slice(640 * q, WIDE if q == 3 else 640 * q + 640)
        store(disco.at[:, spot], disco_any.at[:, spot])
    for copy in stores:
        copy.wait()


def per_device(
    latent,
    member_seeds,
    member_table,
    row_bands,
    disco_basis,
    w_disco,
    w_expand,
    w_reduce,
    w_decode,
    target,
):
    vm = pl.BlockSpec(memory_space=pltpu.VMEM)
    hbm = pl.BlockSpec(memory_space=pltpu.HBM)
    V = pltpu.VMEM
    copies = 180
    scratch = [
        V((2, 45, 4, CH), bf16),
        pltpu.SMEM((2,), jnp.int32),
        V((64, CH), bf16),
        pltpu.SMEM((4,), jnp.int32),
        V((7, 7, 4, 16), bf16),
        V((45, 4, OUTC), bf16),
        V((CH, WIDE), bf16),
        V((CH, HID), bf16),
        V((CH, HID), bf16),
        V((OUTC, CH), bf16),
        V((4, HALF, 256), bf16),
        V((256, 768), bf16),
        V((2, 256, 768), bf16),
        V((ROWS, 768), bf16),
        V((ROWS, 2688), bf16),
        V((ROWS, 768), bf16),
        V((768, ROWS), bf16),
        V((ROWS, HID), f32),
        V((ROWS, 1408), bf16),
        V((ROWS, 768), bf16),
        V((2, 2, 16, 768), bf16),
        V((2, 2, 16, 768), bf16),
        V((8, 48, OUTC), bf16),
        V((8, 48, OUTC), bf16),
        V((16, 24, OUTC), f32),
        V((16, 24, OUTC), f32),
        V((8, 48, OUTC), bf16),
        V((8, 48, OUTC), bf16),
        V((HALF, OUTC), f32),
        V((ROWS, 384), bf16),
        V((ROWS, 768), bf16),
        V((ROWS, 1408), bf16),
        V((ROWS, 768), bf16),
        V((768, CH), bf16),
        V((2, 2, 16, CH), f32),
        V((2, 2, 16, CH), f32),
        V((TILES, 16, 128), bf16),
        V((912, 16, 128), bf16),
        V((684, 16, 128), bf16),
        V((171, 16, 128), bf16),
        V((228, 16, 128), bf16),
        pltpu.SemaphoreType.DMA((copies,)),
        pltpu.SemaphoreType.DMA((copies,)),
        pltpu.SemaphoreType.DMA((10,)),
    ]
    lg, flat = pl.pallas_call(
        step_kernel,
        out_shape=(
            V((2, 45, 4, CH), bf16),
            V((TILES, 16, 128), bf16),
        ),
        in_specs=[hbm] * 10,
        out_specs=(vm, vm),
        scratch_shapes=scratch,
        compiler_params=pltpu.CompilerParams(
            collective_id=0, has_side_effects=True, vmem_limit_bytes=58000000
        ),
        name="step",
    )(
        latent.transpose(0, 2, 1, 3),
        member_seeds,
        member_table,
        row_bands,
        disco_basis.transpose(2, 3, 1, 0),
        w_disco.T,
        w_expand,
        w_reduce.T,
        w_decode.T,
        target.transpose(1, 0, 2),
    )
    shapes = ((CH, WIDE), (CH, HID), (CH, HID), (OUTC, CH), (2, 45, 4, CH))
    disco, expand, reduce, decode, lg = pl.pallas_call(
        unpack_kernel,
        out_shape=tuple(jax.ShapeDtypeStruct(shape, bf16) for shape in shapes),
        in_specs=[vm, vm],
        out_specs=(hbm,) * 5,
        scratch_shapes=[V(shape, bf16) for shape in shapes[:4]]
        + [pltpu.SemaphoreType.DMA((8,))],
        compiler_params=pltpu.CompilerParams(vmem_limit_bytes=24_000_000),
        name="unpack",
    )(flat, lg)
    return (lg.transpose(0, 2, 1, 3), disco.T, expand, reduce.T, decode.T)


def solution(mesh):
    placed = (
        P("member", None, "lon", None),
        P("member"),
        P(),
        P(),
        P(),
        P(),
        P(),
        P(),
        P(),
        P(None, "lon", None),
    )
    return jax.shard_map(
        per_device,
        mesh=mesh,
        in_specs=placed,
        out_specs=(P("member", None, "lon", None), P(), P(), P(), P()),
        check_vma=False,
    )
```

```python
import functools
import math

import jax
import jax.numpy as jnp
from jax import lax
from jax.experimental import pallas as pl
from jax.experimental.pallas import tpu as pltpu
from jax.sharding import PartitionSpec as P

MESH = pl.DeviceIdType.MESH
f32 = jnp.float32
bf16 = jnp.bfloat16

CH = 641
HID = 1282
OUTC = 288
WIDE = 2564
ROWS = 384
HALF = 192
POINTS = 180
UNITS = 41
AXES = (("x", "y", "z"), ("y", "z", "x"), ("z", "x", "y"))
OFF_EXPAND, OFF_REDUCE, OFF_DECODE, OFF_DISCO, OFF_TAIL = 0, 410, 820, 960, 1780
U_DECODE = 18
TILES = 1824
WAVES = ((0, 160), (960, 144))


def place():
    member, lon = lax.axis_index("member"), lax.axis_index("lon")
    return {
        "x": (member % 2) * 2 + (lon // 2) % 2,
        "y": lon // 4,
        "z": member // 2,
        "c": lon % 2,
    }


def device(at):
    return (at["z"] * 2 + at["x"] // 2, at["y"] * 4 + (at["x"] % 2) * 2 + at["c"])


def moved(at, axis, step):
    there = dict(at)
    size = 2 if axis == "c" else 4
    there[axis] = lax.rem(at[axis] + step + size, size)
    return there


def iota(shape, dim):
    return lax.broadcasted_iota(jnp.int32, shape, dim)


def dot(a, b):
    return jnp.dot(a, b, preferred_element_type=f32)


def dot_nt(a, b):
    return lax.dot_general(a, b, (((1,), (1,)), ((), ())), preferred_element_type=f32)


def flat_tiles(value):
    return value.astype(bf16).reshape(value.shape[0] // 16, 16, 128)


class Copies:
    def __init__(self, send_sems, recv_sems):
        self.send_sems, self.recv_sems, self.count = send_sems, recv_sems, 0
        self.started = []

    def send(self, src, dst, to):
        copy = pltpu.make_async_remote_copy(
            src_ref=src,
            dst_ref=dst,
            send_sem=self.send_sems.at[self.count],
            recv_sem=self.recv_sems.at[self.count],
            device_id=to,
            device_id_type=MESH,
        )
        self.count += 1
        copy.start()
        self.started.append(copy)
        return copy

    def finish(self):
        for copy in self.started:
            copy.wait_send()


def pair_slopes(fv, og, tgt, me_h, lanes, rows):
    lo, width = lanes
    values = [fv[j, rows, lo : lo + width] for j in range(16)]
    sums = [None] * 16

    def slope(d):
        return d * lax.rsqrt(d * d + 0.25)

    for i in range(16):
        for j in range(i + 1, 16):
            s = slope(values[i] - values[j])
            sums[i] = s if sums[i] is None else sums[i] + s
            sums[j] = -s if sums[j] is None else sums[j] - s
    goal = tgt[:, lo : lo + width]
    keep = me_h
    for i in range(16):
        value = slope(values[i] - goal) - sums[i] * (1.0 / 15.0)
        og[i, rows, lo : lo + width] = jnp.where(keep, value, 0.0)


def step_kernel(
    latent_any,
    seeds_any,
    table_any,
    bands_any,
    basis_any,
    wd_any,
    we_any,
    wr_any,
    wo_any,
    target_any,
    lg,
    flat,
    latent,
    seeds,
    table,
    bands,
    basis,
    target,
    wd,
    we,
    wr,
    wo,
    tk,
    tt,
    wide,
    hs,
    spread,
    hid,
    hid_t,
    gp,
    act,
    mix,
    halo_s,
    halo_r,
    fs,
    fr,
    fv,
    og,
    gs,
    gr,
    tp,
    fg,
    mg,
    pg,
    hg,
    sgs,
    ob,
    back_r,
    grads,
    r0,
    r1,
    r2,
    r3,
    send_sems,
    recv_sems,
    load_sems,
):
    at = place()
    me = lax.axis_index("member")
    lon = lax.axis_index("lon")
    left = (me, lax.rem(lon + 15, 16))
    right = (me, lax.rem(lon + 1, 16))
    core = at["c"]
    copies = Copies(send_sems, recv_sems)

    early = []
    for i, (src, dst) in enumerate(
        (
            (latent_any, latent),
            (seeds_any, seeds),
            (table_any, table),
            (bands_any, bands),
            (basis_any, basis),
            (target_any, target),
        )
    ):
        load = pltpu.make_async_copy(src, dst, load_sems.at[4 + i])
        load.start()
        early.append(load)
    loads = []
    for i, (src, dst) in enumerate(((wd_any, wd), (we_any, we), (wr_any, wr), (wo_any, wo))):
        load = pltpu.make_async_copy(src, dst, load_sems.at[i])
        load.start()
        loads.append(load)

    sibling = device(moved(at, "c", 1))
    barrier = pltpu.get_barrier_semaphore()
    greet = [sibling, left, right]
    greet += [device(moved(at, axis, d)) for axis in "xyz" for d in (1, 2, 3)]
    greet += [(lax.rem(me + d, 8), lon) for d in range(1, 8)]
    for peer in greet:
        pl.semaphore_signal(barrier, inc=1, device_id=peer, device_id_type=MESH)

    for ref in (hid, mix, mg, hg):
        ref[:, 640:768] = jnp.zeros((ROWS, 128), bf16)
    for ref in (act, pg):
        ref[:, 1280:1408] = jnp.zeros((ROWS, 128), bf16)
    fg[:, 256:384] = jnp.zeros((ROWS, 128), bf16)
    low4 = iota((16, 768), 0) < 4
    for load in early:
        load.wait()
    for m in range(2):
        pick = jnp.where(iota((8, 64), 1) == seeds[m], 1.0, 0.0).astype(bf16)
        offset = dot(pick, table[...])[0:1]
        value = latent[m].astype(f32).reshape(POINTS, CH) + offset
        value = jnp.concatenate([value, jnp.zeros((POINTS, 127), f32)], axis=1)
        value = jnp.concatenate([value, jnp.zeros((76, 768), f32)], axis=0)
        seeded = value.astype(bf16)
        wide[m] = seeded
        hs[m * HALF : m * HALF + HALF] = seeded[0:HALF]
        first = pltpu.roll(value[0:16], 4, 0)
        final = pltpu.roll(value[160:192], 28, 0)[0:16]
        halo_s[0, m] = jnp.where(low4, 0.0, first).astype(bf16)
        halo_s[1, m] = jnp.where(low4, 0.0, final).astype(bf16)

    line = iota((8, 16), 0) & 3
    chosen = jnp.where(line == 0, bands[0], jnp.where(line == 1, bands[1], bands[2]))
    chosen = jnp.where(line == 3, bands[3], chosen)
    picks = jnp.where(iota((8, 16), 1) == chosen, 1.0, 0.0).astype(bf16)
    taps = dot_nt(picks, basis[...].astype(f32).reshape(196, 16).astype(bf16))
    line = iota((8, 196), 0) & 3
    index = iota((8, 196), 1)
    taps = jnp.where((index >= 28 * (3 - line)) & (index < 28 * (7 - line)), taps, 0.0)
    taps = taps.astype(bf16)
    index = iota((196, 256), 0)
    pair = lax.shift_right_logical(index, 2)
    a = lax.shift_right_logical(pair * 37, 8)
    spot = (4 * (pair - 7 * a) + a + (256 - 15)) & 255
    hit = iota((196, 256), 1) == spot
    sub = iota((8, 256), 0)
    def stencil_matrix(k):
        place_k = jnp.where(hit & ((index & 3) == k), 1.0, 0.0).astype(bf16)
        first = pltpu.roll(dot(taps, place_k), 0, 1, stride=1, stride_axis=0)
        lines = [first if i == 0 else pltpu.roll(first, 8 * i, 1) for i in range(23)]
        lines[22] = jnp.where(sub < 4, lines[22], 0.0)
        lines.append(jnp.zeros((8, 256), f32))
        band = jnp.concatenate(lines, axis=0).astype(bf16)
        tk[k] = band

    stencil_matrix(0)
    stencil_matrix(1)
    pl.semaphore_wait(barrier, len(greet))
    from_right = copies.send(halo_s.at[0], halo_r.at[0], left)
    from_left = copies.send(halo_s.at[1], halo_r.at[1], right)
    stencil_matrix(2)
    stencil_matrix(3)

    from_right.wait_recv()
    from_left.wait_recv()
    for m in range(2):
        wide[m, 176:192] = wide[m, 176:192] + halo_r[0, m]
        wide[m, 240:256] = halo_r[1, m]

    for m in range(2):
        carry = None
        rows = slice(m * HALF, m * HALF + HALF)
        for k in range(4):
            value = dot(tk[k], wide[m])
            if k:
                value = pltpu.roll(value, k, 1)
            head = value[:, 0:128] if carry is None else value[:, 0:128] + carry
            spread[rows, 640 * k : 640 * k + 128] = head.astype(bf16)
            spread[rows, 640 * k + 128 : 640 * k + 640] = value[:, 128:640].astype(bf16)
            carry = value[:, 640:768]
        spread[rows, 2560:2688] = carry.astype(bf16)

    for load in loads:
        load.wait()
    conv = dot_nt(spread[:, 0:WIDE], wd[...])
    hid[:, 0:CH] = (hs[:, 0:CH].astype(f32) + conv).astype(bf16)
    pre = dot(hid[:, 0:CH], we[...])
    inner = math.sqrt(2.0 / math.pi)
    gp[...] = pre
    t = jnp.tanh(inner * (pre + 0.044715 * (pre * pre * pre)))
    act[:, 0:HID] = (0.5 * pre * (1.0 + t)).astype(bf16)
    mix[:, 0:CH] = (hid[:, 0:CH].astype(f32) + dot_nt(act[:, 0:HID], wr[...])).astype(bf16)
    fields = dot_nt(mix[:, 0:CH], wo[...])
    for p in range(8):
        block = jnp.concatenate(
            [fields[24 * p : 24 * p + 24], fields[HALF + 24 * p : HALF + 24 * p + 24]], axis=0
        )
        fs[p] = block.astype(bf16)
    there = []
    for d in range(1, 8):
        peer = lax.rem(me + d, 8)
        there.append(copies.send(fs.at[peer], fr.at[me], (peer, lon)))
    fr[me] = fs[me]
    hid_t[...] = hid[...].T
    pre = gp[...]
    square = pre * pre
    t = jnp.tanh(inner * (pre + 0.044715 * (square * pre)))
    gp[...] = 0.5 * (1.0 + t) + (0.5 * inner) * pre * (1.0 - t * t) * (
        1.0 + (3.0 * 0.044715) * square
    )
    for k in range(4):
        tt[:, k * HALF : k * HALF + HALF] = tk[k].T
    tp[0:176] = target[0:44].astype(f32).reshape(176, OUTC)
    tp[176:184] = jnp.concatenate(
        [target[44].astype(f32), jnp.zeros((4, OUTC), f32)], axis=0
    )
    tp[184:192] = jnp.zeros((8, OUTC), f32)

    for copy in there:
        copy.wait_recv()
    for p in range(8):
        block = fr[p].astype(f32)
        fv[2 * p] = block[0:24]
        fv[2 * p + 1] = block[24:48]

    def slopes(i, carry):
        start = pl.multiple_of(i * 8, 8)
        rows = pl.ds(start, 8)
        goal = tp[pl.ds(pl.multiple_of(me * 24 + start, 8), 8), :]
        for lanes in ((0, 128), (128, 128), (256, 32)):
            keep = iota((8, lanes[1]), 0) + (me * 24 + start) < POINTS
            pair_slopes(fv, og, goal, keep, lanes, rows)
        return carry

    lax.fori_loop(0, 3, slopes, 0)
    for p in range(8):
        gs[p] = jnp.concatenate([og[2 * p], og[2 * p + 1]], axis=0).astype(bf16)
    back = []
    for d in range(1, 8):
        peer = lax.rem(me + d, 8)
        back.append(copies.send(gs.at[peer], gr.at[me], (peer, lon)))
    gr[me] = gs[me]
    for copy in back:
        copy.wait_recv()
    blocks = [gr[p].astype(f32) for p in range(8)]
    fg[:, 0:OUTC] = jnp.concatenate(
        [b[0:24] for b in blocks] + [b[24:48] for b in blocks], axis=0
    ).astype(bf16)

    factor = 1.0 / math.sqrt(46080.0)
    def add_tiles(dst, dst_at, parts, count, step, scale=None):
        def body(i, carry):
            total = None
            for ref, start in parts:
                piece = ref[pl.ds(start + i * step, step)].astype(f32)
                total = piece if total is None else total + piece
            if scale is not None:
                total = total * scale
            dst[pl.ds(dst_at + i * step, step)] = total.astype(bf16)
            return carry

        lax.fori_loop(0, count // step, body, 0)

    def reduced(wave, p):
        base, size = WAVES[wave]
        sa, sb = size // 4, size // 16
        start = base + 2 * p * size
        mine = start + core * size
        first, second, third = AXES[p]
        mine_a = mine + at[first] * sa
        mine_b = mine_a + at[second] * sb
        lane = (0 if wave == 0 else 480) + p * size
        r0_at = lane
        lane_a = (0 if wave == 0 else 360) + p * 3 * sa
        lane_b = (0 if wave == 0 else 90) + p * 3 * sb
        lane_c = (0 if wave == 0 else 120) + p * 4 * sb

        def to_peers(axis, src, dst):
            return [
                copies.send(src(d, moved(at, axis, d)), dst(d), device(moved(at, axis, d)))
                for d in (1, 3, 2)
            ]

        half = sa // 2
        onward, backward = device(moved(at, first, 1)), device(moved(at, first, 3))

        def block(step, side):
            return mine + lax.rem(at[first] + step, 4) * sa + side * half

        def landing(step):
            return lane_a + step * half

        across = copies.send(
            grads.at[pl.ds(start + (1 - core) * size, size)],
            r0.at[pl.ds(r0_at, size)],
            sibling,
        )
        yield
        across.wait_recv()
        add_tiles(grads, mine, [(grads, mine), (r0, r0_at)], size, 16)

        def give(at_tile, step, to):
            return copies.send(grads.at[pl.ds(at_tile, half)], r1.at[pl.ds(landing(step), half)], to)

        relay_on = give(block(2, 0), 4, onward)
        relay_back = give(block(2, 1), 5, backward)
        sent = [give(block(1, 1), 1, onward), give(block(3, 0), 2, backward)]
        yield
        relay_on.wait_recv()
        add_tiles(grads, block(1, 0), [(grads, block(1, 0)), (r1, landing(4))], half, half)
        sent.append(give(block(1, 0), 0, onward))
        relay_back.wait_recv()
        add_tiles(grads, block(3, 1), [(grads, block(3, 1)), (r1, landing(5))], half, half)
        sent.append(give(block(3, 1), 3, backward))
        yield
        for copy in sent:
            copy.wait_recv()
        add_tiles(
            grads, mine_a, [(grads, mine_a)] + [(r1, lane_a + d * sa) for d in range(2)], sa, sb
        )
        sent = to_peers(
            second,
            lambda d, to: grads.at[pl.ds(mine_a + to[second] * sb, sb)],
            lambda d: r2.at[pl.ds(lane_b + (d - 1) * sb, sb)],
        )
        yield
        for copy in sent:
            copy.wait_recv()
        add_tiles(
            grads, mine_b, [(grads, mine_b)] + [(r2, lane_b + d * sb) for d in range(3)], sb, sb
        )
        own = pl.ds(lane_c + at[third] * sb, sb)
        sent = to_peers(
            third, lambda d, to: grads.at[pl.ds(mine_b, sb)], lambda d: r3.at[own]
        )
        r3[own] = grads[pl.ds(mine_b, sb)]
        yield
        for copy in sent:
            copy.wait_recv()
        add_tiles(flat, mine_b, [(r3, lane_c + q * sb) for q in range(4)], sb, sb, factor)
        region_b = flat.at[pl.ds(mine_b, sb)]
        sent = to_peers(second, lambda d, to: region_b, lambda d: region_b)
        yield
        for copy in sent:
            copy.wait_recv()

        def pass_on(step, side, to):
            region = flat.at[pl.ds(block(step, side), half)]
            return copies.send(region, region, to)

        def share(step):
            region = flat.at[pl.ds(block(step, 0), sa)]
            return copies.send(region, region, sibling)

        from_before = pass_on(0, 0, onward)
        from_after = pass_on(0, 1, backward)
        rest_before = pass_on(0, 1, onward)
        rest_after = pass_on(0, 0, backward)
        last = [share(0)]
        yield
        from_before.wait_recv()
        far_before = pass_on(3, 0, onward)
        from_after.wait_recv()
        far_after = pass_on(1, 1, backward)
        yield
        rest_before.wait_recv()
        last.append(share(3))
        rest_after.wait_recv()
        last.append(share(1))
        yield
        far_before.wait_recv()
        far_after.wait_recv()
        last.append(share(2))
        yield
        for copy in last:
            copy.wait_recv()
        yield

    one = [reduced(0, p) for p in range(3)]
    two = [reduced(1, p) for p in range(3)]

    def advance(*parts):
        for part in parts:
            next(part)

    def put_columns(value, off, units, count):
        for j in range(count):
            grads[pl.ds(off + j * units, units)] = flat_tiles(
                value[0 : units * 16, 128 * j : 128 * j + 128]
            )

    mixed_grad = dot(fg[:, 0:OUTC], wo[...])
    mg[:, 0:CH] = mixed_grad.astype(bf16)
    pg[:, 0:HID] = (dot(mg[:, 0:CH], wr[...]) * gp[...]).astype(bf16)

    value = dot(hid_t[0:656], pg[...])
    put_columns(value, OFF_EXPAND, UNITS, 10)
    advance(one[0])
    tail = pltpu.roll(value[:, 1280:1408], 4, 1)
    value = dot(mg[...].T[0:656], act[...])
    put_columns(value, OFF_REDUCE, UNITS, 10)
    advance(one[1], one[0])
    tail = tail + pltpu.roll(value[:, 1280:1408], 6, 1)
    value = dot(fg[...].T[0:OUTC], mix[...])
    put_columns(value, OFF_DECODE, U_DECODE, 5)
    last_lane = jnp.concatenate([value[:, 640:768], jnp.zeros((656 - OUTC, 128), f32)], axis=0)
    tail = tail + pltpu.roll(last_lane, 8, 1)
    advance(one[2], one[1])

    hidden_grad = mg[:, 0:CH].astype(f32) + dot_nt(pg[:, 0:HID], we[...])
    hg[:, 0:CH] = hidden_grad.astype(bf16)
    advance(one[2])
    hg_t = hg[...].T[0:656]
    for c in range(5):
        value = dot(hg_t, spread[:, 512 * c : 512 * c + 512])
        put_columns(value, OFF_DISCO + 4 * c * UNITS, UNITS, 4)
        if c == 1:
            advance(two[0], one[0])
        if c == 3:
            advance(two[1], two[0], one[1])
    tail = tail + dot(hg_t, spread[:, 2560:2688])
    put_columns(tail, OFF_TAIL, UNITS, 1)
    advance(two[2], two[1], one[2])

    for m in range(2):
        rows = slice(m * HALF, m * HALF + HALF)
        value = dot(hg[rows, 0:CH], wd[...]).astype(bf16).astype(f32)
        value = jnp.concatenate([value, jnp.zeros((HALF, 124), f32)], axis=1)
        for k in range(4):
            piece = value[:, 640 * k : 640 * k + 768]
            if k:
                piece = pltpu.roll(piece, 768 - k, 1)
            sgs[k * HALF : k * HALF + HALF, :] = piece[:, 0:CH].astype(bf16)
        advance(two[2] if m == 0 else two[0])
        out = dot(tt[...], sgs[...])
        ob[0, m] = out[240:256]
        ob[1, m] = out[176:192]
        gp[rows, 0:CH] = hg[rows, 0:CH].astype(f32) + out[0:HALF]
        if m == 0:
            advance(one[0])
    to_left = copies.send(ob.at[0], back_r.at[0], left)
    to_right = copies.send(ob.at[1], back_r.at[1], right)
    advance(one[1], two[1], one[2], two[2], one[0])
    to_left.wait_recv()
    to_right.wait_recv()
    low = iota((16, CH), 0)
    for m in range(2):
        base = m * HALF
        after = pltpu.roll(back_r[1, m], 12, 0)
        gp[base : base + 16, 0:CH] = gp[base : base + 16, 0:CH] + jnp.where(low < 12, after, 0.0)
        before = jnp.where(low >= 4, back_r[0, m], 0.0)
        before = jnp.concatenate([before, jnp.zeros((16, CH), f32)], axis=0)
        before = pltpu.roll(before, 4, 0)
        spot = slice(base + 160, base + 192)
        gp[spot, 0:CH] = gp[spot, 0:CH] + before
        total = gp[base : base + HALF, 0:CH]
        lg[m] = total[0:POINTS].reshape(45, 4, CH).astype(bf16)
    advance(one[1], one[2])
    for _ in range(6):
        advance(*two)
        advance(*one)
    advance(*two)
    advance(*two)
    copies.finish()


def unpack_kernel(
    flat,
    lg,
    disco_any,
    expand_any,
    reduce_any,
    decode_any,
    lg_out,
    disco,
    expand,
    reduce,
    decode,
    out_sems,
):
    stores = []

    def store(src, dst):
        stores.append(pltpu.make_async_copy(src, dst, out_sems.at[len(stores)]))
        stores[-1].start()

    store(lg, lg_out)

    def column(start, units):
        return flat[start : start + units].reshape(units * 16, 128)

    tail = column(OFF_TAIL, UNITS)
    wide_tail = tail.astype(f32)
    for j in range(10):
        expand[:, 128 * j : 128 * j + 128] = column(OFF_EXPAND + j * UNITS, UNITS)[0:CH]
    expand[:, 1280:HID] = pltpu.roll(wide_tail, 124, 1)[0:CH, 0:2].astype(bf16)
    store(expand, expand_any)
    for j in range(10):
        reduce[:, 128 * j : 128 * j + 128] = column(OFF_REDUCE + j * UNITS, UNITS)[0:CH]
    reduce[:, 1280:HID] = pltpu.roll(wide_tail, 122, 1)[0:CH, 0:2].astype(bf16)
    store(reduce, reduce_any)
    for j in range(5):
        decode[:, 128 * j : 128 * j + 128] = column(OFF_DECODE + j * U_DECODE, U_DECODE)
    decode[:, 640:CH] = pltpu.roll(wide_tail, 120, 1)[0:OUTC, 0:1].astype(bf16)
    store(decode, decode_any)
    disco[:, 2560:WIDE] = tail[0:CH, 0:4]
    for q in range(4):
        for j in range(5 * q, 5 * q + 5):
            disco[:, 128 * j : 128 * j + 128] = column(OFF_DISCO + j * UNITS, UNITS)[0:CH]
        spot = slice(640 * q, WIDE if q == 3 else 640 * q + 640)
        store(disco.at[:, spot], disco_any.at[:, spot])
    for copy in stores:
        copy.wait()


def per_device(
    latent,
    member_seeds,
    member_table,
    row_bands,
    disco_basis,
    w_disco,
    w_expand,
    w_reduce,
    w_decode,
    target,
):
    vm = pl.BlockSpec(memory_space=pltpu.VMEM)
    hbm = pl.BlockSpec(memory_space=pltpu.HBM)
    V = pltpu.VMEM
    copies = 180
    scratch = [
        V((2, 45, 4, CH), bf16),
        pltpu.SMEM((2,), jnp.int32),
        V((64, CH), bf16),
        pltpu.SMEM((4,), jnp.int32),
        V((7, 7, 4, 16), bf16),
        V((45, 4, OUTC), bf16),
        V((CH, WIDE), bf16),
        V((CH, HID), bf16),
        V((CH, HID), bf16),
        V((OUTC, CH), bf16),
        V((4, HALF, 256), bf16),
        V((256, 768), bf16),
        V((2, 256, 768), bf16),
        V((ROWS, 768), bf16),
        V((ROWS, 2688), bf16),
        V((ROWS, 768), bf16),
        V((768, ROWS), bf16),
        V((ROWS, HID), f32),
        V((ROWS, 1408), bf16),
        V((ROWS, 768), bf16),
        V((2, 2, 16, 768), bf16),
        V((2, 2, 16, 768), bf16),
        V((8, 48, OUTC), bf16),
        V((8, 48, OUTC), bf16),
        V((16, 24, OUTC), f32),
        V((16, 24, OUTC), f32),
        V((8, 48, OUTC), bf16),
        V((8, 48, OUTC), bf16),
        V((HALF, OUTC), f32),
        V((ROWS, 384), bf16),
        V((ROWS, 768), bf16),
        V((ROWS, 1408), bf16),
        V((ROWS, 768), bf16),
        V((768, CH), bf16),
        V((2, 2, 16, CH), f32),
        V((2, 2, 16, CH), f32),
        V((TILES, 16, 128), bf16),
        V((912, 16, 128), bf16),
        V((684, 16, 128), bf16),
        V((171, 16, 128), bf16),
        V((228, 16, 128), bf16),
        pltpu.SemaphoreType.DMA((copies,)),
        pltpu.SemaphoreType.DMA((copies,)),
        pltpu.SemaphoreType.DMA((10,)),
    ]
    lg, flat = pl.pallas_call(
        step_kernel,
        out_shape=(
            V((2, 45, 4, CH), bf16),
            V((TILES, 16, 128), bf16),
        ),
        in_specs=[hbm] * 10,
        out_specs=(vm, vm),
        scratch_shapes=scratch,
        compiler_params=pltpu.CompilerParams(
            collective_id=0, has_side_effects=True, vmem_limit_bytes=58000000
        ),
        name="step",
    )(
        latent.transpose(0, 2, 1, 3),
        member_seeds,
        member_table,
        row_bands,
        disco_basis.transpose(2, 3, 1, 0),
        w_disco.T,
        w_expand,
        w_reduce.T,
        w_decode.T,
        target.transpose(1, 0, 2),
    )
    shapes = ((CH, WIDE), (CH, HID), (CH, HID), (OUTC, CH), (2, 45, 4, CH))
    disco, expand, reduce, decode, lg = pl.pallas_call(
        unpack_kernel,
        out_shape=tuple(jax.ShapeDtypeStruct(shape, bf16) for shape in shapes),
        in_specs=[vm, vm],
        out_specs=(hbm,) * 5,
        scratch_shapes=[V(shape, bf16) for shape in shapes[:4]]
        + [pltpu.SemaphoreType.DMA((8,))],
        compiler_params=pltpu.CompilerParams(vmem_limit_bytes=24_000_000),
        name="unpack",
    )(flat, lg)
    return (lg.transpose(0, 2, 1, 3), disco.T, expand, reduce.T, decode.T)


def solution(mesh):
    placed = (
        P("member", None, "lon", None),
        P("member"),
        P(),
        P(),
        P(),
        P(),
        P(),
        P(),
        P(),
        P(None, "lon", None),
    )
    return jax.shard_map(
        per_device,
        mesh=mesh,
        in_specs=placed,
        out_specs=(P("member", None, "lon", None), P(), P(), P(), P()),
        check_vma=False,
    )
```

```python
import functools
import math

import jax
import jax.numpy as jnp
from jax import lax
from jax.experimental import pallas as pl
from jax.experimental.pallas import tpu as pltpu
from jax.sharding import PartitionSpec as P

MESH = pl.DeviceIdType.MESH
f32 = jnp.float32
bf16 = jnp.bfloat16

CH = 641
HID = 1282
OUTC = 288
WIDE = 2564
ROWS = 384
HALF = 192
POINTS = 180
UNITS = 41
AXES = (("x", "y", "z"), ("y", "z", "x"), ("z", "x", "y"))
OFF_EXPAND, OFF_REDUCE, OFF_DECODE, OFF_DISCO, OFF_TAIL = 0, 410, 820, 960, 1780
U_DECODE = 18
TILES = 1824
WAVES = ((0, 160), (960, 144))


def place():
    member, lon = lax.axis_index("member"), lax.axis_index("lon")
    return {
        "x": (member % 2) * 2 + (lon // 2) % 2,
        "y": lon // 4,
        "z": member // 2,
        "c": lon % 2,
    }


def device(at):
    return (at["z"] * 2 + at["x"] // 2, at["y"] * 4 + (at["x"] % 2) * 2 + at["c"])


def moved(at, axis, step):
    there = dict(at)
    size = 2 if axis == "c" else 4
    there[axis] = lax.rem(at[axis] + step + size, size)
    return there


def iota(shape, dim):
    return lax.broadcasted_iota(jnp.int32, shape, dim)


def dot(a, b):
    return jnp.dot(a, b, preferred_element_type=f32)


def dot_nt(a, b):
    return lax.dot_general(a, b, (((1,), (1,)), ((), ())), preferred_element_type=f32)


def flat_tiles(value):
    return value.astype(bf16).reshape(value.shape[0] // 16, 16, 128)


def put_block(ref, p, block):
    for i in range(3):
        for j in range(2):
            ref[p, 2 * i + j] = block[16 * i : 16 * i + 16, 128 * j : 128 * j + 128].astype(bf16)
    ends = [block[16 * i : 16 * i + 16, 256:OUTC] for i in range(3)]
    ref[p, 6] = jnp.concatenate(ends + [jnp.zeros((16, 32), f32)], axis=1).astype(bf16)


def take_block(ref, p):
    columns = [
        jnp.concatenate([ref[p, 2 * i + j].astype(f32) for i in range(3)], axis=0)
        for j in range(2)
    ]
    ends = ref[p, 6].astype(f32)
    parts = [ends if i == 0 else pltpu.roll(ends, 128 - 32 * i, 1) for i in range(3)]
    return columns + [jnp.concatenate(parts, axis=0)[:, 0:32]]


class Copies:
    def __init__(self, send_sems, recv_sems):
        self.send_sems, self.recv_sems, self.count = send_sems, recv_sems, 0
        self.started = []

    def send(self, src, dst, to):
        copy = pltpu.make_async_remote_copy(
            src_ref=src,
            dst_ref=dst,
            send_sem=self.send_sems.at[self.count],
            recv_sem=self.recv_sems.at[self.count],
            device_id=to,
            device_id_type=MESH,
        )
        self.count += 1
        copy.start()
        self.started.append(copy)
        return copy

    def finish(self):
        for copy in self.started:
            copy.wait_send()


def pair_slopes(fv, og, tgt, me_h, lanes, rows):
    lo, width = lanes
    values = [fv[j, rows, lo : lo + width] for j in range(16)]
    sums = [None] * 16

    def slope(d):
        return d * lax.rsqrt(d * d + 0.25)

    for i in range(16):
        for j in range(i + 1, 16):
            s = slope(values[i] - values[j])
            sums[i] = s if sums[i] is None else sums[i] + s
            sums[j] = -s if sums[j] is None else sums[j] - s
    goal = tgt[:, lo : lo + width]
    keep = me_h
    for i in range(16):
        value = slope(values[i] - goal) - sums[i] * (1.0 / 15.0)
        og[i, rows, lo : lo + width] = jnp.where(keep, value, 0.0)


def step_kernel(
    latent_any,
    seeds_any,
    table_any,
    bands_any,
    basis_any,
    wd_any,
    we_any,
    wr_any,
    wo_any,
    target_any,
    lg,
    flat,
    latent,
    seeds,
    table,
    bands,
    basis,
    target,
    wd,
    we,
    wr,
    wo,
    tk,
    tt,
    wide,
    hs,
    spread,
    hid,
    hid_t,
    gp,
    act,
    mix,
    halo_s,
    halo_r,
    fs,
    fr,
    fv,
    og,
    gs,
    gr,
    tp,
    fg,
    mg,
    pg,
    hg,
    sgs,
    ob,
    back_r,
    grads,
    r0,
    r1,
    r2,
    r3,
    send_sems,
    recv_sems,
    load_sems,
):
    at = place()
    me = lax.axis_index("member")
    lon = lax.axis_index("lon")
    left = (me, lax.rem(lon + 15, 16))
    right = (me, lax.rem(lon + 1, 16))
    core = at["c"]
    copies = Copies(send_sems, recv_sems)

    early = []
    for i, (src, dst) in enumerate(
        (
            (latent_any, latent),
            (seeds_any, seeds),
            (table_any, table),
            (bands_any, bands),
            (basis_any, basis),
            (target_any, target),
        )
    ):
        load = pltpu.make_async_copy(src, dst, load_sems.at[4 + i])
        load.start()
        early.append(load)
    loads = []
    for i, (src, dst) in enumerate(((wd_any, wd), (we_any, we), (wr_any, wr), (wo_any, wo))):
        load = pltpu.make_async_copy(src, dst, load_sems.at[i])
        load.start()
        loads.append(load)

    sibling = device(moved(at, "c", 1))
    barrier = pltpu.get_barrier_semaphore()
    greet = [sibling, left, right]
    greet += [device(moved(at, axis, d)) for axis in "xyz" for d in (1, 2, 3)]
    greet += [(lax.rem(me + d, 8), lon) for d in range(1, 8)]
    for peer in greet:
        pl.semaphore_signal(barrier, inc=1, device_id=peer, device_id_type=MESH)

    for ref in (hid, mix, mg, hg):
        ref[:, 640:768] = jnp.zeros((ROWS, 128), bf16)
    for ref in (act, pg):
        ref[:, 1280:1408] = jnp.zeros((ROWS, 128), bf16)
    fg[:, 256:384] = jnp.zeros((ROWS, 128), bf16)
    low4 = iota((16, 768), 0) < 4
    for load in early:
        load.wait()
    for m in range(2):
        pick = jnp.where(iota((8, 64), 1) == seeds[m], 1.0, 0.0).astype(bf16)
        offset = dot(pick, table[...])[0:1]
        value = latent[m].astype(f32).reshape(POINTS, CH) + offset
        value = jnp.concatenate([value, jnp.zeros((POINTS, 127), f32)], axis=1)
        value = jnp.concatenate([value, jnp.zeros((76, 768), f32)], axis=0)
        seeded = value.astype(bf16)
        wide[m] = seeded
        hs[m * HALF : m * HALF + HALF] = seeded[0:HALF]
        first = pltpu.roll(value[0:16], 4, 0)
        final = pltpu.roll(value[160:192], 28, 0)[0:16]
        halo_s[0, m] = jnp.where(low4, 0.0, first).astype(bf16)
        halo_s[1, m] = jnp.where(low4, 0.0, final).astype(bf16)

    line = iota((8, 16), 0) & 3
    chosen = jnp.where(line == 0, bands[0], jnp.where(line == 1, bands[1], bands[2]))
    chosen = jnp.where(line == 3, bands[3], chosen)
    picks = jnp.where(iota((8, 16), 1) == chosen, 1.0, 0.0).astype(bf16)
    taps = dot_nt(picks, basis[...].astype(f32).reshape(196, 16).astype(bf16))
    line = iota((8, 196), 0) & 3
    index = iota((8, 196), 1)
    taps = jnp.where((index >= 28 * (3 - line)) & (index < 28 * (7 - line)), taps, 0.0)
    taps = taps.astype(bf16)
    index = iota((196, 256), 0)
    pair = lax.shift_right_logical(index, 2)
    a = lax.shift_right_logical(pair * 37, 8)
    spot = (4 * (pair - 7 * a) + a + (256 - 15)) & 255
    hit = iota((196, 256), 1) == spot
    sub = iota((8, 256), 0)
    def stencil_matrix(k):
        place_k = jnp.where(hit & ((index & 3) == k), 1.0, 0.0).astype(bf16)
        first = pltpu.roll(dot(taps, place_k), 0, 1, stride=1, stride_axis=0)
        lines = [first if i == 0 else pltpu.roll(first, 8 * i, 1) for i in range(23)]
        lines[22] = jnp.where(sub < 4, lines[22], 0.0)
        lines.append(jnp.zeros((8, 256), f32))
        band = jnp.concatenate(lines, axis=0).astype(bf16)
        tk[k] = band

    stencil_matrix(0)
    stencil_matrix(1)
    pl.semaphore_wait(barrier, len(greet))
    from_right = copies.send(halo_s.at[0], halo_r.at[0], left)
    from_left = copies.send(halo_s.at[1], halo_r.at[1], right)
    stencil_matrix(2)
    stencil_matrix(3)

    from_right.wait_recv()
    from_left.wait_recv()
    for m in range(2):
        wide[m, 176:192] = wide[m, 176:192] + halo_r[0, m]
        wide[m, 240:256] = halo_r[1, m]

    for m in range(2):
        carry = None
        rows = slice(m * HALF, m * HALF + HALF)
        for k in range(4):
            value = dot(tk[k], wide[m])
            if k:
                value = pltpu.roll(value, k, 1)
            head = value[:, 0:128] if carry is None else value[:, 0:128] + carry
            spread[rows, 640 * k : 640 * k + 128] = head.astype(bf16)
            spread[rows, 640 * k + 128 : 640 * k + 640] = value[:, 128:640].astype(bf16)
            carry = value[:, 640:768]
        spread[rows, 2560:2688] = carry.astype(bf16)

    for load in loads:
        load.wait()
    conv = dot_nt(spread[:, 0:WIDE], wd[...])
    hid[:, 0:CH] = (hs[:, 0:CH].astype(f32) + conv).astype(bf16)
    pre = dot(hid[:, 0:CH], we[...])
    inner = math.sqrt(2.0 / math.pi)
    gp[...] = pre
    t = jnp.tanh(inner * (pre + 0.044715 * (pre * pre * pre)))
    act[:, 0:HID] = (0.5 * pre * (1.0 + t)).astype(bf16)
    mix[:, 0:CH] = (hid[:, 0:CH].astype(f32) + dot_nt(act[:, 0:HID], wr[...])).astype(bf16)
    fields = dot_nt(mix[:, 0:CH], wo[...])
    for p in range(8):
        block = jnp.concatenate(
            [fields[24 * p : 24 * p + 24], fields[HALF + 24 * p : HALF + 24 * p + 24]], axis=0
        )
        put_block(fs, p, block)
    there = []
    for d in range(1, 8):
        peer = lax.rem(me + d, 8)
        there.append(copies.send(fs.at[peer], fr.at[me], (peer, lon)))
    fr[me] = fs[me]
    hid_t[...] = hid[...].T
    pre = gp[...]
    square = pre * pre
    t = jnp.tanh(inner * (pre + 0.044715 * (square * pre)))
    gp[...] = 0.5 * (1.0 + t) + (0.5 * inner) * pre * (1.0 - t * t) * (
        1.0 + (3.0 * 0.044715) * square
    )
    for k in range(4):
        tt[:, k * HALF : k * HALF + HALF] = tk[k].T
    tp[0:176] = target[0:44].astype(f32).reshape(176, OUTC)
    tp[176:184] = jnp.concatenate(
        [target[44].astype(f32), jnp.zeros((4, OUTC), f32)], axis=0
    )
    tp[184:192] = jnp.zeros((8, OUTC), f32)

    for copy in there:
        copy.wait_recv()
    for p in range(8):
        for lo, piece in zip((0, 128, 256), take_block(fr, p)):
            wide_to = slice(lo, min(lo + 128, OUTC))
            fv[2 * p, :, wide_to] = piece[0:24]
            fv[2 * p + 1, :, wide_to] = piece[24:48]

    def slopes(i, carry):
        start = pl.multiple_of(i * 8, 8)
        rows = pl.ds(start, 8)
        goal = tp[pl.ds(pl.multiple_of(me * 24 + start, 8), 8), :]
        for lanes in ((0, 128), (128, 128), (256, 32)):
            keep = iota((8, lanes[1]), 0) + (me * 24 + start) < POINTS
            pair_slopes(fv, og, goal, keep, lanes, rows)
        return carry

    lax.fori_loop(0, 3, slopes, 0)
    for p in range(8):
        put_block(gs, p, jnp.concatenate([og[2 * p], og[2 * p + 1]], axis=0))
    back = []
    for d in range(1, 8):
        peer = lax.rem(me + d, 8)
        back.append(copies.send(gs.at[peer], gr.at[me], (peer, lon)))
    gr[me] = gs[me]
    for copy in back:
        copy.wait_recv()
    blocks = [take_block(gr, p) for p in range(8)]
    for q, lo in enumerate((0, 128, 256)):
        pieces = [b[q][0:24] for b in blocks] + [b[q][24:48] for b in blocks]
        fg[:, lo : min(lo + 128, OUTC)] = jnp.concatenate(pieces, axis=0).astype(bf16)

    factor = 1.0 / math.sqrt(46080.0)
    def add_tiles(dst, dst_at, parts, count, step, scale=None):
        def body(i, carry):
            total = None
            for ref, start in parts:
                piece = ref[pl.ds(start + i * step, step)].astype(f32)
                total = piece if total is None else total + piece
            if scale is not None:
                total = total * scale
            dst[pl.ds(dst_at + i * step, step)] = total.astype(bf16)
            return carry

        lax.fori_loop(0, count // step, body, 0)

    def reduced(wave, p):
        base, size = WAVES[wave]
        sa, sb = size // 4, size // 16
        start = base + 2 * p * size
        mine = start + core * size
        first, second, third = AXES[p]
        mine_a = mine + at[first] * sa
        mine_b = mine_a + at[second] * sb
        lane = (0 if wave == 0 else 480) + p * size
        r0_at = lane
        lane_a = (0 if wave == 0 else 360) + p * 3 * sa
        lane_b = (0 if wave == 0 else 90) + p * 3 * sb
        lane_c = (0 if wave == 0 else 120) + p * 4 * sb

        def to_peers(axis, src, dst):
            return [
                copies.send(src(d, moved(at, axis, d)), dst(d), device(moved(at, axis, d)))
                for d in (1, 3, 2)
            ]

        half = sa // 2
        onward, backward = device(moved(at, first, 1)), device(moved(at, first, 3))

        def block(step, side):
            return mine + lax.rem(at[first] + step, 4) * sa + side * half

        def landing(step):
            return lane_a + step * half

        across = copies.send(
            grads.at[pl.ds(start + (1 - core) * size, size)],
            r0.at[pl.ds(r0_at, size)],
            sibling,
        )
        yield
        across.wait_recv()
        add_tiles(grads, mine, [(grads, mine), (r0, r0_at)], size, 16)

        def give(at_tile, step, to):
            return copies.send(grads.at[pl.ds(at_tile, half)], r1.at[pl.ds(landing(step), half)], to)

        relay_on = give(block(2, 0), 4, onward)
        relay_back = give(block(2, 1), 5, backward)
        sent = [give(block(1, 1), 1, onward), give(block(3, 0), 2, backward)]
        yield
        relay_on.wait_recv()
        add_tiles(grads, block(1, 0), [(grads, block(1, 0)), (r1, landing(4))], half, half)
        sent.append(give(block(1, 0), 0, onward))
        relay_back.wait_recv()
        add_tiles(grads, block(3, 1), [(grads, block(3, 1)), (r1, landing(5))], half, half)
        sent.append(give(block(3, 1), 3, backward))
        yield
        for copy in sent:
            copy.wait_recv()
        add_tiles(
            grads, mine_a, [(grads, mine_a)] + [(r1, lane_a + d * sa) for d in range(2)], sa, sb
        )
        sent = to_peers(
            second,
            lambda d, to: grads.at[pl.ds(mine_a + to[second] * sb, sb)],
            lambda d: r2.at[pl.ds(lane_b + (d - 1) * sb, sb)],
        )
        yield
        for copy in sent:
            copy.wait_recv()
        add_tiles(
            grads, mine_b, [(grads, mine_b)] + [(r2, lane_b + d * sb) for d in range(3)], sb, sb
        )
        own = pl.ds(lane_c + at[third] * sb, sb)
        sent = to_peers(
            third, lambda d, to: grads.at[pl.ds(mine_b, sb)], lambda d: r3.at[own]
        )
        r3[own] = grads[pl.ds(mine_b, sb)]
        yield
        for copy in sent:
            copy.wait_recv()
        add_tiles(flat, mine_b, [(r3, lane_c + q * sb) for q in range(4)], sb, sb, factor)
        region_b = flat.at[pl.ds(mine_b, sb)]
        sent = to_peers(second, lambda d, to: region_b, lambda d: region_b)
        yield
        for copy in sent:
            copy.wait_recv()

        def pass_on(step, side, to):
            region = flat.at[pl.ds(block(step, side), half)]
            return copies.send(region, region, to)

        def share(step):
            region = flat.at[pl.ds(block(step, 0), sa)]
            return copies.send(region, region, sibling)

        from_before = pass_on(0, 0, onward)
        from_after = pass_on(0, 1, backward)
        rest_before = pass_on(0, 1, onward)
        rest_after = pass_on(0, 0, backward)
        last = [share(0)]
        yield
        from_before.wait_recv()
        far_before = pass_on(3, 0, onward)
        from_after.wait_recv()
        far_after = pass_on(1, 1, backward)
        yield
        rest_before.wait_recv()
        last.append(share(3))
        rest_after.wait_recv()
        last.append(share(1))
        yield
        far_before.wait_recv()
        far_after.wait_recv()
        last.append(share(2))
        yield
        for copy in last:
            copy.wait_recv()
        yield

    one = [reduced(0, p) for p in range(3)]
    two = [reduced(1, p) for p in range(3)]

    def advance(*parts):
        for part in parts:
            next(part)

    def put_columns(value, off, units, count):
        for j in range(count):
            grads[pl.ds(off + j * units, units)] = flat_tiles(
                value[0 : units * 16, 128 * j : 128 * j + 128]
            )

    mixed_grad = dot(fg[:, 0:OUTC], wo[...])
    mg[:, 0:CH] = mixed_grad.astype(bf16)
    pg[:, 0:HID] = (dot(mg[:, 0:CH], wr[...]) * gp[...]).astype(bf16)

    value = dot(hid_t[0:656], pg[...])
    put_columns(value, OFF_EXPAND, UNITS, 10)
    advance(one[0])
    tail = pltpu.roll(value[:, 1280:1408], 4, 1)
    value = dot(mg[...].T[0:656], act[...])
    put_columns(value, OFF_REDUCE, UNITS, 10)
    advance(one[1], one[0])
    tail = tail + pltpu.roll(value[:, 1280:1408], 6, 1)
    value = dot(fg[...].T[0:OUTC], mix[...])
    put_columns(value, OFF_DECODE, U_DECODE, 5)
    last_lane = jnp.concatenate([value[:, 640:768], jnp.zeros((656 - OUTC, 128), f32)], axis=0)
    tail = tail + pltpu.roll(last_lane, 8, 1)
    advance(one[2], one[1])

    hidden_grad = mg[:, 0:CH].astype(f32) + dot_nt(pg[:, 0:HID], we[...])
    hg[:, 0:CH] = hidden_grad.astype(bf16)
    advance(one[2])
    hg_t = hg[...].T[0:656]
    for c in range(5):
        value = dot(hg_t, spread[:, 512 * c : 512 * c + 512])
        put_columns(value, OFF_DISCO + 4 * c * UNITS, UNITS, 4)
        if c == 1:
            advance(two[0], one[0])
        if c == 3:
            advance(two[1], two[0], one[1])
    tail = tail + dot(hg_t, spread[:, 2560:2688])
    put_columns(tail, OFF_TAIL, UNITS, 1)
    advance(two[2], two[1], one[2])

    for m in range(2):
        rows = slice(m * HALF, m * HALF + HALF)
        value = dot(hg[rows, 0:CH], wd[...]).astype(bf16).astype(f32)
        value = jnp.concatenate([value, jnp.zeros((HALF, 124), f32)], axis=1)
        for k in range(4):
            piece = value[:, 640 * k : 640 * k + 768]
            if k:
                piece = pltpu.roll(piece, 768 - k, 1)
            sgs[k * HALF : k * HALF + HALF, :] = piece[:, 0:CH].astype(bf16)
        advance(two[2] if m == 0 else two[0])
        out = dot(tt[...], sgs[...])
        ob[0, m] = out[240:256]
        ob[1, m] = out[176:192]
        gp[rows, 0:CH] = hg[rows, 0:CH].astype(f32) + out[0:HALF]
        if m == 0:
            advance(one[0])
    to_left = copies.send(ob.at[0], back_r.at[0], left)
    to_right = copies.send(ob.at[1], back_r.at[1], right)
    advance(one[1], two[1], one[2], two[2], one[0])
    to_left.wait_recv()
    to_right.wait_recv()
    low = iota((16, CH), 0)
    for m in range(2):
        base = m * HALF
        after = pltpu.roll(back_r[1, m], 12, 0)
        gp[base : base + 16, 0:CH] = gp[base : base + 16, 0:CH] + jnp.where(low < 12, after, 0.0)
        before = jnp.where(low >= 4, back_r[0, m], 0.0)
        before = jnp.concatenate([before, jnp.zeros((16, CH), f32)], axis=0)
        before = pltpu.roll(before, 4, 0)
        spot = slice(base + 160, base + 192)
        gp[spot, 0:CH] = gp[spot, 0:CH] + before
        total = gp[base : base + HALF, 0:CH]
        lg[m] = total[0:POINTS].reshape(45, 4, CH).astype(bf16)
    advance(one[1], one[2])
    for _ in range(6):
        advance(*two)
        advance(*one)
    advance(*two)
    advance(*two)
    copies.finish()


def unpack_kernel(
    flat,
    lg,
    disco_any,
    expand_any,
    reduce_any,
    decode_any,
    lg_out,
    disco,
    expand,
    reduce,
    decode,
    out_sems,
):
    stores = []

    def store(src, dst):
        stores.append(pltpu.make_async_copy(src, dst, out_sems.at[len(stores)]))
        stores[-1].start()

    store(lg, lg_out)

    def column(start, units):
        return flat[start : start + units].reshape(units * 16, 128)

    tail = column(OFF_TAIL, UNITS)
    wide_tail = tail.astype(f32)
    for j in range(10):
        expand[:, 128 * j : 128 * j + 128] = column(OFF_EXPAND + j * UNITS, UNITS)[0:CH]
    expand[:, 1280:HID] = pltpu.roll(wide_tail, 124, 1)[0:CH, 0:2].astype(bf16)
    store(expand, expand_any)
    for j in range(10):
        reduce[:, 128 * j : 128 * j + 128] = column(OFF_REDUCE + j * UNITS, UNITS)[0:CH]
    reduce[:, 1280:HID] = pltpu.roll(wide_tail, 122, 1)[0:CH, 0:2].astype(bf16)
    store(reduce, reduce_any)
    for j in range(5):
        decode[:, 128 * j : 128 * j + 128] = column(OFF_DECODE + j * U_DECODE, U_DECODE)
    decode[:, 640:CH] = pltpu.roll(wide_tail, 120, 1)[0:OUTC, 0:1].astype(bf16)
    store(decode, decode_any)
    disco[:, 2560:WIDE] = tail[0:CH, 0:4]
    for q in range(4):
        for j in range(5 * q, 5 * q + 5):
            disco[:, 128 * j : 128 * j + 128] = column(OFF_DISCO + j * UNITS, UNITS)[0:CH]
        spot = slice(640 * q, WIDE if q == 3 else 640 * q + 640)
        store(disco.at[:, spot], disco_any.at[:, spot])
    for copy in stores:
        copy.wait()


def per_device(
    latent,
    member_seeds,
    member_table,
    row_bands,
    disco_basis,
    w_disco,
    w_expand,
    w_reduce,
    w_decode,
    target,
):
    vm = pl.BlockSpec(memory_space=pltpu.VMEM)
    hbm = pl.BlockSpec(memory_space=pltpu.HBM)
    V = pltpu.VMEM
    copies = 180
    scratch = [
        V((2, 45, 4, CH), bf16),
        pltpu.SMEM((2,), jnp.int32),
        V((64, CH), bf16),
        pltpu.SMEM((4,), jnp.int32),
        V((7, 7, 4, 16), bf16),
        V((45, 4, OUTC), bf16),
        V((CH, WIDE), bf16),
        V((CH, HID), bf16),
        V((CH, HID), bf16),
        V((OUTC, CH), bf16),
        V((4, HALF, 256), bf16),
        V((256, 768), bf16),
        V((2, 256, 768), bf16),
        V((ROWS, 768), bf16),
        V((ROWS, 2688), bf16),
        V((ROWS, 768), bf16),
        V((768, ROWS), bf16),
        V((ROWS, HID), f32),
        V((ROWS, 1408), bf16),
        V((ROWS, 768), bf16),
        V((2, 2, 16, 768), bf16),
        V((2, 2, 16, 768), bf16),
        V((8, 7, 16, 128), bf16),
        V((8, 7, 16, 128), bf16),
        V((16, 24, OUTC), f32),
        V((16, 24, OUTC), f32),
        V((8, 7, 16, 128), bf16),
        V((8, 7, 16, 128), bf16),
        V((HALF, OUTC), f32),
        V((ROWS, 384), bf16),
        V((ROWS, 768), bf16),
        V((ROWS, 1408), bf16),
        V((ROWS, 768), bf16),
        V((768, CH), bf16),
        V((2, 2, 16, CH), f32),
        V((2, 2, 16, CH), f32),
        V((TILES, 16, 128), bf16),
        V((912, 16, 128), bf16),
        V((684, 16, 128), bf16),
        V((171, 16, 128), bf16),
        V((228, 16, 128), bf16),
        pltpu.SemaphoreType.DMA((copies,)),
        pltpu.SemaphoreType.DMA((copies,)),
        pltpu.SemaphoreType.DMA((10,)),
    ]
    lg, flat = pl.pallas_call(
        step_kernel,
        out_shape=(
            V((2, 45, 4, CH), bf16),
            V((TILES, 16, 128), bf16),
        ),
        in_specs=[hbm] * 10,
        out_specs=(vm, vm),
        scratch_shapes=scratch,
        compiler_params=pltpu.CompilerParams(
            collective_id=0, has_side_effects=True, vmem_limit_bytes=58000000
        ),
        name="step",
    )(
        latent.transpose(0, 2, 1, 3),
        member_seeds,
        member_table,
        row_bands,
        disco_basis.transpose(2, 3, 1, 0),
        w_disco.T,
        w_expand,
        w_reduce.T,
        w_decode.T,
        target.transpose(1, 0, 2),
    )
    shapes = ((CH, WIDE), (CH, HID), (CH, HID), (OUTC, CH), (2, 45, 4, CH))
    disco, expand, reduce, decode, lg = pl.pallas_call(
        unpack_kernel,
        out_shape=tuple(jax.ShapeDtypeStruct(shape, bf16) for shape in shapes),
        in_specs=[vm, vm],
        out_specs=(hbm,) * 5,
        scratch_shapes=[V(shape, bf16) for shape in shapes[:4]]
        + [pltpu.SemaphoreType.DMA((8,))],
        compiler_params=pltpu.CompilerParams(vmem_limit_bytes=24_000_000),
        name="unpack",
    )(flat, lg)
    return (lg.transpose(0, 2, 1, 3), disco.T, expand, reduce.T, decode.T)


def solution(mesh):
    placed = (
        P("member", None, "lon", None),
        P("member"),
        P(),
        P(),
        P(),
        P(),
        P(),
        P(),
        P(),
        P(None, "lon", None),
    )
    return jax.shard_map(
        per_device,
        mesh=mesh,
        in_specs=placed,
        out_specs=(P("member", None, "lon", None), P(), P(), P(), P()),
        check_vma=False,
    )
```
